768 devices in a mesh: rows: 64 (over x, y, core), ang: 12 (over z).
Axes of the slice: x: 4, y: 8, z: 12, core: 2. Of those that a mesh axis runs over, the one named last changes fastest.
Arguments:
- delta_obj: float32 [8704, 2, 1536], P('rows', None, 'ang'), may hold values from -4 to 4
- beta_obj: float32 [8704, 2, 1536], P('rows', None, 'ang'), may hold values from 0 to 0.15
- layer_shifts: int32 [12, 2], replicated, may hold values from -8 to 8
- illumination_field: float32 [2, 128, 128], replicated, may hold values from -6 to 6
- amplitudes: float32 [12, 256, 128, 128], P('ang', 'rows'), may hold values from 0.2 to 3
- positions: int32 [12, 256, 2], P('ang', 'rows'), may hold values from 0 to 1408, as said below
- scan_counts: int32 [12, 64], P('ang', 'rows'), may hold values from 1 to 4, as said below
Outputs:
- grad_delta: float32 [8704, 2, 1536], P('rows', None, 'ang')
- grad_beta: float32 [8704, 2, 1536], P('rows', None, 'ang')
The draws below stay inside these ranges and needn't reach their ends.
Inputs may be any that keep to these rules, and one draw needn't show every extreme that they name: `positions`: within each tile at each angle the slots come in order: a first group, at most 1 of them, has row offsets above 8; all later slots have row offsets of at most 8. Columns are at most 1408. `scan_counts`: slots of a tile from this number on are not used.
All inputs are finite; a program needn't handle non-finite values.
Results may differ from the reference program's by a relative error of at most 0.0046.
Values may be sent and summed in bfloat16 or wider, within the bound.
A program may use at most 32 MiB of HBM per device.

```python
import math
import jax
import jax.numpy as jnp
from jax import lax

PATTERN_PIXELS = 128
TH = 136
COLS_DEV = 128
LAYERS = 2
SHIFT = 8
SCAN_SLOT_LIMIT = 4
EDGE_CAP = 1
TILE_COUNT = 64
ANGLES = 12
HEIGHT = 8704
WIDTH = 1536
SCANS = 256
N_ANG = 12


def scan_plan(key):
    keys = jax.random.split(jax.random.fold_in(key, 11), 9)
    grid_shape = (ANGLES, TILE_COUNT)
    rare = jax.random.randint(keys[0], grid_shape, 0, 8) == 0
    heavy = jax.random.randint(keys[1], grid_shape, SCAN_SLOT_LIMIT // 2, SCAN_SLOT_LIMIT + 1)
    light = jax.random.randint(keys[2], grid_shape, 1, SCAN_SLOT_LIMIT // 2 + 1)
    scan_totals = jnp.where(rare, heavy, light)
    pick_angle = jax.random.randint(keys[3], (), 0, ANGLES)
    pick_tile = jax.random.randint(keys[4], (), 0, TILE_COUNT)
    chosen = (jnp.arange(ANGLES)[:, None] == pick_angle) & (jnp.arange(TILE_COUNT)[None, :] == pick_tile)
    scan_totals = jnp.where(chosen, SCAN_SLOT_LIMIT, scan_totals)
    edges = jnp.minimum(jax.random.randint(keys[5], grid_shape, 0, EDGE_CAP + 1), scan_totals)
    edges = jnp.where(chosen, EDGE_CAP, edges)
    return (scan_totals.astype(jnp.int32), edges.astype(jnp.int32), chosen, keys)


def draw_scan_counts(key, part):
    scan_totals, edges, chosen, keys = scan_plan(key)
    return scan_totals


def draw_positions(key, part):
    scan_totals, edges, chosen, keys = scan_plan(key)
    slot_ids = jnp.arange(SCAN_SLOT_LIMIT)
    full_shape = (ANGLES, TILE_COUNT, SCAN_SLOT_LIMIT)
    is_edge = slot_ids[None, None, :] < edges[:, :, None]
    inner = jax.random.randint(keys[6], full_shape, 0, TH - PATTERN_PIXELS + 1)
    outer = jax.random.randint(keys[7], full_shape, TH - PATTERN_PIXELS + 1, TH)
    row_off = jnp.where(is_edge, outer, inner)
    col_off = jax.random.randint(keys[8], full_shape, 0, WIDTH - PATTERN_PIXELS + 1)
    first = chosen[:, :, None] & (slot_ids == 0)[None, None, :]
    row_off = jnp.where(first, TH - 1, row_off)
    col_off = jnp.where(first, WIDTH - PATTERN_PIXELS, col_off)
    return jnp.stack([row_off, col_off], -1).reshape(ANGLES, SCANS, 2).astype(jnp.int32)


def draw_layer_shifts(key, part):
    shifts = jax.random.randint(jax.random.fold_in(key, 23), (ANGLES, LAYERS), -SHIFT, SHIFT + 1)
    shifts = shifts.at[0, 0].set(SHIFT)
    shifts = shifts.at[0, 1].set(-SHIFT)
    return shifts.astype(jnp.int32)


def level_of(own_key, dims, cuts, least, largest):
    def one(dim, parts):
        heights = jax.random.uniform(jax.random.fold_in(jax.random.fold_in(own_key, 6), dim), (parts,), jnp.float32, least / len(cuts), largest / len(cuts))
        return jnp.repeat(jnp.exp(heights), dims[dim] // parts).reshape((-1,) + (1,) * (len(dims) - dim - 1))

    level = one(*cuts[0])
    for cut in cuts[1:]:
        level = level * one(*cut)
    return level


def gaussian(rng, extent, width, bound, cuts=(), held_as=jnp.bfloat16):
    loudness = level_of(rng, extent, cuts, -0.22, 0.18) if cuts else 1.0
    entries = jax.random.normal(rng, extent, jnp.float32) * width * loudness
    return jnp.minimum(jnp.maximum(entries, -bound), bound).astype(held_as)


def setup_inputs(seed: int = 0) -> dict:
    key_list = jax.random.split(jax.random.key(seed), 8)
    delta_obj = gaussian(key_list[0], (HEIGHT, LAYERS, WIDTH), 0.3, 4.0, ((0, 64), (2, 12)), jnp.float32)
    beta_obj = jnp.clip(0.15 * jax.random.uniform(key_list[1], (HEIGHT, LAYERS, WIDTH), jnp.float32) ** level_of(key_list[1], (HEIGHT, LAYERS, WIDTH), ((0, 64), (2, 12)), -0.2, 0.2), 0.0, 0.15)
    layer_shifts = draw_layer_shifts(jax.random.fold_in(key_list[7], 71), 0)
    illumination_field = gaussian(key_list[3], (2, PATTERN_PIXELS, PATTERN_PIXELS), 1.0, 6.0, (), jnp.float32)
    amplitudes = jnp.clip(jnp.exp(math.log(3.0) - 2.7080502 * jax.random.uniform(key_list[4], (ANGLES, SCANS, PATTERN_PIXELS, PATTERN_PIXELS), jnp.float32) ** level_of(key_list[4], (ANGLES, SCANS, PATTERN_PIXELS, PATTERN_PIXELS), ((0, 12), (1, 64)), -0.2, 0.2)), 0.2, 3.0)
    positions = draw_positions(jax.random.fold_in(key_list[7], 71), 0)
    scan_counts = draw_scan_counts(jax.random.fold_in(key_list[7], 71), 0)
    return dict(delta_obj=delta_obj, beta_obj=beta_obj, layer_shifts=layer_shifts, illumination_field=illumination_field, amplitudes=amplitudes, positions=positions, scan_counts=scan_counts)


best_prec = lax.Precision.HIGHEST
amp_floor = 0.1

def dft_tables():
    counter = jnp.arange(PATTERN_PIXELS, dtype=jnp.int32)
    product = counter[:, None] * counter[None, :] % PATTERN_PIXELS
    angle_table = product.astype(jnp.float32) * (2.0 * math.pi / PATTERN_PIXELS)
    factor = 1.0 / math.sqrt(PATTERN_PIXELS)
    return (jnp.cos(angle_table) * factor, -jnp.sin(angle_table) * factor)

def transform(real_in, imag_in, fourier_real, fourier_imaginary):
    left_re = jnp.matmul(fourier_real, real_in, precision=best_prec) - jnp.matmul(fourier_imaginary, imag_in, precision=best_prec)
    left_im = jnp.matmul(fourier_real, imag_in, precision=best_prec) + jnp.matmul(fourier_imaginary, real_in, precision=best_prec)
    out_re = jnp.matmul(left_re, fourier_real, precision=best_prec) - jnp.matmul(left_im, fourier_imaginary, precision=best_prec)
    out_im = jnp.matmul(left_re, fourier_imaginary, precision=best_prec) + jnp.matmul(left_im, fourier_real, precision=best_prec)
    return (out_re, out_im)

def scan_gradients(object_patches, illumination_field, measured_patterns, misfit_weight, fourier_real, fourier_imaginary):
    probe_re = illumination_field[0]
    probe_im = illumination_field[1]
    patch_re = object_patches[:, 0]
    patch_im = object_patches[:, 1]
    exit_re = probe_re * patch_re - probe_im * patch_im
    exit_im = probe_re * patch_im + probe_im * patch_re
    far_re, far_im = transform(exit_re, exit_im, fourier_real, fourier_imaginary)
    modulus = jnp.sqrt(far_re * far_re + far_im * far_im)
    factor = (1.0 - measured_patterns / jnp.maximum(modulus, amp_floor)) * misfit_weight[:, None, None]
    back_re, back_im = transform(far_re * factor, far_im * factor, fourier_real, -fourier_imaginary)
    return jnp.stack([probe_re * back_re + probe_im * back_im, probe_re * back_im - probe_im * back_re], axis=1)

def transmit(phase_in, absorb_in):
    damping = jnp.exp(-absorb_in)
    return (damping * jnp.cos(phase_in), damping * jnp.sin(phase_in))

def chain_back(trans_re, trans_im, grad_re, grad_im):
    return (trans_re * grad_im - trans_im * grad_re, -(trans_re * grad_re + trans_im * grad_im))

def assemble(windows, columns, margin):
    leading = windows.shape[:2]
    groups = windows.shape[2]
    full_width = groups * columns
    main_part = windows[..., :columns].reshape(leading + (full_width,))
    tail_part = jnp.pad(windows[..., columns:], ((0, 0), (0, 0), (0, 0), (0, columns - 2 * margin)))
    tail_part = tail_part.reshape(leading + (full_width,))
    padding = jnp.zeros(leading + (columns,), windows.dtype)
    extended = jnp.concatenate([main_part, padding], -1) + jnp.concatenate([padding, tail_part], -1)
    result = extended[..., margin:margin + full_width]
    result = result.at[..., full_width - margin:].add(extended[..., :margin])
    result = result.at[..., :columns - margin].add(extended[..., full_width + margin:])
    return result

def cut_windows(gradient, columns, margin):
    leading = gradient.shape[:2]
    full_width = gradient.shape[2]
    groups = full_width // columns
    extended = jnp.concatenate([gradient[..., full_width - margin:], gradient, gradient[..., :columns - margin]], -1)
    main_part = extended[..., :full_width].reshape(leading + (groups, columns))
    tail_part = extended[..., columns:full_width + columns].reshape(leading + (groups, columns))[..., :2 * margin]
    return jnp.concatenate([main_part, tail_part], -1)

def scan_angle(transmission, measured_patterns, spot_list, scan_totals, illumination_field, fourier_real, fourier_imaginary):
    tile_measured = measured_patterns.reshape(TILE_COUNT, SCAN_SLOT_LIMIT, PATTERN_PIXELS, PATTERN_PIXELS)
    tile_positions = spot_list.reshape(TILE_COUNT, SCAN_SLOT_LIMIT, 2)

    def tile_update(grad_trans, input_bundle):
        tile_index, measured_tile, position_tile, active_count = input_bundle
        row_start = tile_index * TH + position_tile[:, 0]
        col_start = position_tile[:, 1]
        object_patches = jax.vmap(lambda r_pos, c_pos: lax.dynamic_slice(transmission, (jnp.int32(0), r_pos, c_pos), (2, PATTERN_PIXELS, PATTERN_PIXELS)))(row_start, col_start)
        misfit_weight = (jnp.arange(SCAN_SLOT_LIMIT, dtype=jnp.int32) < active_count).astype(jnp.float32)
        patch_gradient = scan_gradients(object_patches, illumination_field, measured_tile, misfit_weight, fourier_real, fourier_imaginary)

        def add_one(slot_idx, total):
            anchor = (jnp.int32(0), row_start[slot_idx], col_start[slot_idx])
            current = lax.dynamic_slice(total, anchor, (2, PATTERN_PIXELS, PATTERN_PIXELS))
            return lax.dynamic_update_slice(total, current + patch_gradient[slot_idx], anchor)
        return (lax.fori_loop(0, SCAN_SLOT_LIMIT, add_one, grad_trans), None)
    tile_numbers = jnp.arange(TILE_COUNT, dtype=jnp.int32)
    return lax.scan(tile_update, jnp.zeros_like(transmission), (tile_numbers, tile_measured, tile_positions, scan_totals))[0]

def reference(delta_obj, beta_obj, layer_shifts, illumination_field, amplitudes, positions, scan_counts):
    height, layers, full_width = delta_obj.shape
    window_len = COLS_DEV + 2 * SHIFT
    blocks = jnp.stack([delta_obj, beta_obj]).reshape(2, height, layers, N_ANG, COLS_DEV)
    blocks = jnp.pad(blocks, ((0, 0), (0, 0), (0, 0), (0, 0), (2 * SHIFT, 2 * SHIFT)))
    fourier_real, fourier_imaginary = dft_tables()

    def angle_step(grad_obj, input_bundle):
        shift_row, measured_patterns, spot_list, scan_totals = input_bundle

        def add_layer(layer_idx, total):
            layer_slab = lax.dynamic_index_in_dim(blocks, layer_idx, 2, keepdims=False)
            return total + lax.dynamic_slice_in_dim(layer_slab, SHIFT + shift_row[layer_idx], window_len, 3)
        windows = lax.fori_loop(0, layers, add_layer, jnp.zeros((2, height, N_ANG, window_len), jnp.float32))
        windows = lax.optimization_barrier(windows.astype(jnp.bfloat16)).astype(jnp.float32)
        projection = assemble(windows, COLS_DEV, SHIFT)
        extended = jnp.pad(projection, ((0, 0), (0, PATTERN_PIXELS), (0, 0)))
        trans_re, trans_im = transmit(extended[0], extended[1])
        grad_trans = scan_angle(jnp.stack([trans_re, trans_im]), measured_patterns, spot_list, scan_totals, illumination_field, fourier_real, fourier_imaginary)
        grad_phase, grad_absorb = chain_back(trans_re, trans_im, grad_trans[0], grad_trans[1])
        grad_proj = jnp.stack([grad_phase, grad_absorb])[:, :height]
        grad_win = cut_windows(grad_proj, COLS_DEV, SHIFT)
        grad_win = lax.optimization_barrier(grad_win.astype(jnp.bfloat16)).astype(jnp.float32)

        def back_layer(layer_idx, total):
            layer_part = lax.dynamic_slice_in_dim(grad_win, SHIFT - shift_row[layer_idx], COLS_DEV, 3)
            layer_part = layer_part.reshape(2, height, full_width)
            current = lax.dynamic_index_in_dim(total, layer_idx, 2, keepdims=False)
            return lax.dynamic_update_index_in_dim(total, current + layer_part, layer_idx, 2)
        return (lax.fori_loop(0, layers, back_layer, grad_obj), None)
    start_grad = jnp.zeros((2, height, layers, full_width), jnp.float32)
    grad_obj = lax.scan(angle_step, start_grad, (layer_shifts, amplitudes, positions, scan_counts))[0]
    return (grad_obj[0], grad_obj[1])
```

```python
import functools
import math

import jax
import jax.numpy as jnp
import numpy as np
from jax import lax
from jax.experimental import pallas as pl
from jax.experimental.pallas import tpu as pltpu
from jax.sharding import PartitionSpec as P

PIX = 128
TH = 136
COLS = 128
LAYERS = 2
SHIFT = 8
SLOTS = 4
AMP_FLOOR = 0.1
BLOCK_ROWS = 2 * LAYERS * TH
CHAN_ROWS = LAYERS * TH
F32 = jnp.float32
BF16 = jnp.bfloat16


def dft_constants():
    counter = np.arange(PIX)
    angle = (counter[:, None] * counter[None, :] % PIX) * (2.0 * math.pi / PIX)
    scale = 1.0 / math.sqrt(PIX)
    re = np.cos(angle) * scale
    im = -np.sin(angle) * scale
    m1 = np.block([[re, -im], [im, re]])
    m2 = np.block([[re, im], [-im, re]])

    def split(m):
        hi = m.astype(BF16)
        lo = (m - hi.astype(np.float64)).astype(BF16)
        return np.asarray(hi), np.asarray(lo)

    return split(m1) + split(m2)


def split_f32(x):
    hi = x.astype(BF16)
    lo = (x - hi.astype(F32)).astype(BF16)
    return hi, lo


def dot(a, b):
    return jnp.dot(a, b, preferred_element_type=F32)


def left_product(hi, lo, data):
    d_hi, d_lo = split_f32(data)
    return dot(hi, d_hi) + (dot(hi, d_lo) + dot(lo, d_hi))


def right_product(data, hi, lo):
    d_hi, d_lo = split_f32(data)
    return dot(d_hi, hi) + (dot(d_lo, hi) + dot(d_hi, lo))


def sin_cos(x):
    k = jnp.floor(x * (2.0 / math.pi) + 0.5)
    y = x - k * 1.5703125
    y = y - k * 4.837512969970703125e-4
    y = y - k * 7.54978995489188216e-8
    q = k.astype(jnp.int32)
    y2 = y * y
    s = y + y * y2 * (-1.6666654611e-1 + y2 * (8.3321608736e-3 + y2 * -1.9515295891e-4))
    c = (1.0 - 0.5 * y2) + y2 * y2 * (
        4.166664568298827e-2 + y2 * (-1.388731625493765e-3 + y2 * 2.443315711809948e-5)
    )
    odd = (q & 1) == 1
    sn = jnp.where(odd, c, s)
    cs = jnp.where(odd, s, c)
    sn = jnp.where((q & 2) == 2, -sn, sn)
    cs = jnp.where(((q + 1) & 2) == 2, -cs, cs)
    return sn, cs


def place(col, shift, blocks):
    start = col + shift
    start = jnp.where(start < 0, start + blocks * COLS, start)
    first = jnp.right_shift(start, 7)
    offset = start & (COLS - 1)
    second = jnp.where(first == blocks - 1, 0, first + 1)
    return first, second, offset


def lanes(rows):
    return lax.broadcasted_iota(jnp.int32, (rows, COLS), 1)


def read_strip(g_ref, chan, col, shifts_ref, angle, blocks):
    total = None
    lane = lanes(TH)
    for z in range(LAYERS):
        first, second, offset = place(col, shifts_ref[angle, z], blocks)
        rows = pl.ds(chan * CHAN_ROWS, CHAN_ROWS)
        part0 = g_ref[first, rows, :].astype(F32)[z * TH : (z + 1) * TH]
        part1 = g_ref[second, rows, :].astype(F32)[z * TH : (z + 1) * TH]
        both = jnp.where(lane >= offset, part0, part1)
        strip = pltpu.roll(both, (COLS - offset) & (COLS - 1), 1)
        total = strip if total is None else total + strip
    return total


def halo_kernel(blocks, g_ref, shifts_ref, prev_ref, out_ref):
    angle = lax.axis_index("ang")
    col = jnp.clip(prev_ref[0, 1], 0, blocks * COLS - PIX)
    for chan in range(2):
        out_ref[chan] = read_strip(g_ref, chan, col, shifts_ref, angle, blocks)[:PIX]


def slot_row(pos_ref, slot):
    return jnp.clip(pos_ref[0, slot, 0], 0, TH if slot == 0 else TH - PIX)


def slot_col(pos_ref, slot, blocks):
    return jnp.clip(pos_ref[0, slot, 1], 0, blocks * COLS - PIX)


def scan_kernel(
    blocks,
    g_ref,
    halo_ref,
    field_ref,
    amp_ref,
    m1h_ref,
    m1l_ref,
    m2h_ref,
    m2l_ref,
    shifts_ref,
    pos_ref,
    count_ref,
    grad_ref,
    down_ref,
    strip_ref,
    trans_ref,
    back_ref,
):
    angle = lax.axis_index("ang")
    probe_re = field_ref[0]
    probe_im = field_ref[1]
    exit_re, exit_im = [], []
    for slot in range(SLOTS):
        col = slot_col(pos_ref, slot, blocks)
        row = slot_row(pos_ref, slot)
        for chan in range(2):
            strip_ref[slot, chan, :TH] = read_strip(g_ref, chan, col, shifts_ref, angle, blocks)
            if slot == 0:
                strip_ref[slot, chan, TH:] = halo_ref[chan]
        phase = strip_ref[slot, 0, pl.ds(row, PIX), :]
        damping = jnp.exp(-strip_ref[slot, 1, pl.ds(row, PIX), :])
        sn, cs = sin_cos(phase)
        tre = damping * cs
        tim = damping * sn
        trans_ref[slot, 0] = tre
        trans_ref[slot, 1] = tim
        exit_re.append(probe_re * tre - probe_im * tim)
        exit_im.append(probe_re * tim + probe_im * tre)
    data = jnp.concatenate(
        [jnp.concatenate(exit_re, axis=1), jnp.concatenate(exit_im, axis=1)], axis=0
    )
    left = left_product(m1h_ref[...], m1l_ref[...], data)
    wide = jnp.concatenate(
        [
            jnp.concatenate(
                [left[:PIX, j * PIX : (j + 1) * PIX], left[PIX:, j * PIX : (j + 1) * PIX]], axis=1
            )
            for j in range(SLOTS)
        ],
        axis=0,
    )
    far = right_product(wide, m2h_ref[...], m2l_ref[...])
    residual = []
    for slot in range(SLOTS):
        rows = far[slot * PIX : (slot + 1) * PIX]
        re, im = rows[:, :PIX], rows[:, PIX:]
        live = (slot < count_ref[0, 0]).astype(F32)
        inverse = lax.rsqrt(jnp.maximum(re * re + im * im, AMP_FLOOR * AMP_FLOOR))
        factor = (1.0 - amp_ref[0, slot] * inverse) * live
        residual.append(jnp.concatenate([re * factor, im * factor], axis=1))
    back = right_product(jnp.concatenate(residual, axis=0), m1h_ref[...], m1l_ref[...])
    tall = jnp.concatenate(
        [
            jnp.concatenate([back[j * PIX : (j + 1) * PIX, :PIX] for j in range(SLOTS)], axis=1),
            jnp.concatenate([back[j * PIX : (j + 1) * PIX, PIX:] for j in range(SLOTS)], axis=1),
        ],
        axis=0,
    )
    grad = left_product(m2h_ref[...], m2l_ref[...], tall)
    for slot in range(SLOTS):
        bre = grad[:PIX, slot * PIX : (slot + 1) * PIX]
        bim = grad[PIX:, slot * PIX : (slot + 1) * PIX]
        gre = probe_re * bre + probe_im * bim
        gim = probe_re * bim - probe_im * bre
        tre = trans_ref[slot, 0]
        tim = trans_ref[slot, 1]
        row = slot_row(pos_ref, slot)
        total_rows = TH + PIX if slot == 0 else TH
        for chan, value in enumerate((tre * gim - tim * gre, -(tre * gre + tim * gim))):
            back_ref[chan, :total_rows] = jnp.zeros((total_rows, PIX), F32)
            back_ref[chan, pl.ds(row, PIX), :] = value
            grad_ref[slot, chan] = back_ref[chan, :TH]
            if slot == 0:
                down_ref[chan] = back_ref[chan, TH:]


def spread_kernel(blocks, grad_ref, up_ref, shifts_ref, pos_ref, prev_ref, out_ref, acc_ref):
    angle = lax.axis_index("ang")
    acc_ref[...] = jnp.zeros_like(acc_ref)
    lane = lanes(TH)
    for slot in range(SLOTS + 1):
        if slot < SLOTS:
            col = slot_col(pos_ref, slot, blocks)
        else:
            col = jnp.clip(prev_ref[0, 1], 0, blocks * COLS - PIX)
        for chan in range(2):
            if slot < SLOTS:
                value = grad_ref[slot, chan]
            else:
                value = jnp.concatenate([up_ref[chan], jnp.zeros((TH - PIX, PIX), F32)], axis=0)
            for z in range(LAYERS):
                first, second, offset = place(col, shifts_ref[angle, z], blocks)
                rolled = pltpu.roll(value, offset, 1)
                rows = pl.ds(chan * CHAN_ROWS + z * TH, TH)
                acc_ref[first, rows, :] += jnp.where(lane >= offset, rolled, 0.0)
                acc_ref[second, rows, :] += jnp.where(lane < offset, rolled, 0.0)
    for b in range(blocks):
        out_ref[b] = acc_ref[b].astype(BF16)


VMEM = pl.BlockSpec(memory_space=pltpu.VMEM)
SMEM = pl.BlockSpec(memory_space=pltpu.SMEM)
PARAMS = pltpu.CompilerParams(vmem_limit_bytes=48 << 20)


def shift_rows(value, steps):
    count = lax.axis_size("rows")
    first, last = max(0, -steps), min(count, count - steps)
    return lax.ppermute(value, "rows", [(i, i + steps) for i in range(first, last)])


def on_device(delta_obj, beta_obj, layer_shifts, field, amplitudes, positions, counts):
    blocks = lax.axis_size("ang")
    m1h, m1l, m2h, m2l = dft_constants()
    prev = shift_rows(positions[0, :1], 1)
    own = jnp.concatenate(
        [obj[:, z, :].astype(BF16) for obj in (delta_obj, beta_obj) for z in range(LAYERS)], axis=0
    )
    gathered = lax.all_gather(own, "ang")
    strip = pl.pallas_call(
        functools.partial(halo_kernel, blocks),
        out_shape=jax.ShapeDtypeStruct((2, PIX, PIX), F32),
        in_specs=[VMEM, SMEM, SMEM],
        out_specs=VMEM,
        compiler_params=PARAMS,
    )(gathered, layer_shifts, prev)
    halo = shift_rows(strip, -1)
    grads, down = pl.pallas_call(
        functools.partial(scan_kernel, blocks),
        out_shape=(
            jax.ShapeDtypeStruct((SLOTS, 2, TH, PIX), F32),
            jax.ShapeDtypeStruct((2, PIX, PIX), F32),
        ),
        in_specs=[VMEM] * 8 + [SMEM] * 3,
        out_specs=(VMEM, VMEM),
        scratch_shapes=[
            pltpu.VMEM((SLOTS, 2, TH + PIX, PIX), F32),
            pltpu.VMEM((SLOTS, 2, PIX, PIX), F32),
            pltpu.VMEM((2, TH + PIX, PIX), F32),
        ],
        compiler_params=PARAMS,
    )(gathered, halo, field, amplitudes, m1h, m1l, m2h, m2l, layer_shifts, positions, counts)
    up = shift_rows(down, 1)
    spread = pl.pallas_call(
        functools.partial(spread_kernel, blocks),
        out_shape=jax.ShapeDtypeStruct((blocks, BLOCK_ROWS, COLS), BF16),
        in_specs=[VMEM, VMEM, SMEM, SMEM, SMEM],
        out_specs=VMEM,
        scratch_shapes=[pltpu.VMEM((blocks, BLOCK_ROWS, COLS), F32)],
        compiler_params=PARAMS,
    )(grads, up, layer_shifts, positions, prev)
    total = lax.psum_scatter(spread, "ang", scatter_dimension=0)
    total = total.astype(F32).reshape(2, LAYERS, TH, COLS)
    total = jnp.transpose(total, (0, 2, 1, 3))
    return (total[0], total[1])


def solution(mesh):
    placed = (
        P("rows", None, "ang"),
        P("rows", None, "ang"),
        P(),
        P(),
        P("ang", "rows", None, None),
        P("ang", "rows", None),
        P("ang", "rows"),
    )
    return jax.shard_map(
        on_device,
        mesh=mesh,
        in_specs=placed,
        out_specs=(P("rows", None, "ang"), P("rows", None, "ang")),
        check_vma=False,
    )
```

```python
import functools
import math

import jax
import jax.numpy as jnp
import numpy as np
from jax import lax
from jax.experimental import pallas as pl
from jax.experimental.pallas import tpu as pltpu
from jax.sharding import PartitionSpec as P

PIX = 128
TH = 136
COLS = 128
LAYERS = 2
SHIFT = 8
SLOTS = 4
AMP_FLOOR = 0.1
BLOCK_ROWS = 2 * LAYERS * TH
CHAN_ROWS = LAYERS * TH
F32 = jnp.float32
BF16 = jnp.bfloat16


def dft_constants():
    counter = np.arange(PIX)
    angle = (counter[:, None] * counter[None, :] % PIX) * (2.0 * math.pi / PIX)
    scale = 1.0 / math.sqrt(PIX)
    re = np.cos(angle) * scale
    im = -np.sin(angle) * scale
    m1 = np.block([[re, -im], [im, re]])
    m2 = np.block([[re, im], [-im, re]])

    def split(m):
        hi = m.astype(BF16)
        lo = (m - hi.astype(np.float64)).astype(BF16)
        return np.asarray(hi), np.asarray(lo)

    return split(m1) + split(m2)


def split_f32(x):
    hi = x.astype(BF16)
    lo = (x - hi.astype(F32)).astype(BF16)
    return hi, lo


def dot(a, b):
    return jnp.dot(a, b, preferred_element_type=F32)


def left_product(hi, lo, data):
    d_hi, d_lo = split_f32(data)
    return dot(hi, d_hi) + (dot(hi, d_lo) + dot(lo, d_hi))


def right_product(data, hi, lo):
    d_hi, d_lo = split_f32(data)
    return dot(d_hi, hi) + (dot(d_lo, hi) + dot(d_hi, lo))


def sin_cos(x):
    k = jnp.floor(x * (2.0 / math.pi) + 0.5)
    y = x - k * 1.5703125
    y = y - k * 4.837512969970703125e-4
    y = y - k * 7.54978995489188216e-8
    q = k.astype(jnp.int32)
    y2 = y * y
    s = y + y * y2 * (-1.6666654611e-1 + y2 * (8.3321608736e-3 + y2 * -1.9515295891e-4))
    c = (1.0 - 0.5 * y2) + y2 * y2 * (
        4.166664568298827e-2 + y2 * (-1.388731625493765e-3 + y2 * 2.443315711809948e-5)
    )
    odd = (q & 1) == 1
    sn = jnp.where(odd, c, s)
    cs = jnp.where(odd, s, c)
    sn = jnp.where((q & 2) == 2, -sn, sn)
    cs = jnp.where(((q + 1) & 2) == 2, -cs, cs)
    return sn, cs


def place(col, shift, blocks):
    start = col + shift
    start = jnp.where(start < 0, start + blocks * COLS, start)
    first = jnp.right_shift(start, 7)
    offset = start & (COLS - 1)
    second = jnp.where(first == blocks - 1, 0, first + 1)
    return first, second, offset


def lanes(rows):
    return lax.broadcasted_iota(jnp.int32, (rows, COLS), 1)


def read_strip(g_ref, chan, col, shifts_ref, angle, blocks):
    total = None
    lane = lanes(TH)
    for z in range(LAYERS):
        first, second, offset = place(col, shifts_ref[angle, z], blocks)
        rows = pl.ds(chan * CHAN_ROWS, CHAN_ROWS)
        part0 = g_ref[first, rows, :].astype(F32)[z * TH : (z + 1) * TH]
        part1 = g_ref[second, rows, :].astype(F32)[z * TH : (z + 1) * TH]
        both = jnp.where(lane >= offset, part0, part1)
        strip = pltpu.roll(both, (COLS - offset) & (COLS - 1), 1)
        total = strip if total is None else total + strip
    return total


def halo_kernel(blocks, g_ref, shifts_ref, prev_ref, out_ref):
    angle = lax.axis_index("ang")
    col = jnp.clip(prev_ref[0, 1], 0, blocks * COLS - PIX)
    for chan in range(2):
        out_ref[chan] = read_strip(g_ref, chan, col, shifts_ref, angle, blocks)[:PIX]


def slot_row(pos_ref, slot):
    return jnp.clip(pos_ref[0, slot, 0], 0, TH if slot == 0 else TH - PIX)


def slot_col(pos_ref, slot, blocks):
    return jnp.clip(pos_ref[0, slot, 1], 0, blocks * COLS - PIX)


def scan_kernel(
    blocks,
    g_ref,
    halo_ref,
    field_ref,
    amp_ref,
    m1h_ref,
    m1l_ref,
    m2h_ref,
    m2l_ref,
    shifts_ref,
    pos_ref,
    count_ref,
    grad_ref,
    down_ref,
    strip_ref,
    trans_ref,
    back_ref,
):
    angle = lax.axis_index("ang")
    probe_re = field_ref[0]
    probe_im = field_ref[1]
    exit_re, exit_im = [], []
    for slot in range(SLOTS):
        col = slot_col(pos_ref, slot, blocks)
        row = slot_row(pos_ref, slot)
        for chan in range(2):
            strip_ref[slot, chan, :TH] = read_strip(g_ref, chan, col, shifts_ref, angle, blocks)
            if slot == 0:
                strip_ref[slot, chan, TH:] = halo_ref[chan]
        phase = strip_ref[slot, 0, pl.ds(row, PIX), :]
        damping = jnp.exp(-strip_ref[slot, 1, pl.ds(row, PIX), :])
        sn, cs = sin_cos(phase)
        tre = damping * cs
        tim = damping * sn
        trans_ref[slot, 0] = tre
        trans_ref[slot, 1] = tim
        exit_re.append(probe_re * tre - probe_im * tim)
        exit_im.append(probe_re * tim + probe_im * tre)
    data = jnp.concatenate(
        [jnp.concatenate(exit_re, axis=1), jnp.concatenate(exit_im, axis=1)], axis=0
    )
    left = left_product(m1h_ref[...], m1l_ref[...], data)
    wide = jnp.concatenate(
        [
            jnp.concatenate(
                [left[:PIX, j * PIX : (j + 1) * PIX], left[PIX:, j * PIX : (j + 1) * PIX]], axis=1
            )
            for j in range(SLOTS)
        ],
        axis=0,
    )
    far = right_product(wide, m2h_ref[...], m2l_ref[...])
    residual = []
    for slot in range(SLOTS):
        rows = far[slot * PIX : (slot + 1) * PIX]
        re, im = rows[:, :PIX], rows[:, PIX:]
        live = (slot < count_ref[0, 0]).astype(F32)
        inverse = lax.rsqrt(jnp.maximum(re * re + im * im, AMP_FLOOR * AMP_FLOOR))
        factor = (1.0 - amp_ref[0, slot] * inverse) * live
        residual.append(jnp.concatenate([re * factor, im * factor], axis=1))
    back = right_product(jnp.concatenate(residual, axis=0), m1h_ref[...], m1l_ref[...])
    tall = jnp.concatenate(
        [
            jnp.concatenate([back[j * PIX : (j + 1) * PIX, :PIX] for j in range(SLOTS)], axis=1),
            jnp.concatenate([back[j * PIX : (j + 1) * PIX, PIX:] for j in range(SLOTS)], axis=1),
        ],
        axis=0,
    )
    grad = left_product(m2h_ref[...], m2l_ref[...], tall)
    for slot in range(SLOTS):
        bre = grad[:PIX, slot * PIX : (slot + 1) * PIX]
        bim = grad[PIX:, slot * PIX : (slot + 1) * PIX]
        gre = probe_re * bre + probe_im * bim
        gim = probe_re * bim - probe_im * bre
        tre = trans_ref[slot, 0]
        tim = trans_ref[slot, 1]
        row = slot_row(pos_ref, slot)
        total_rows = TH + PIX if slot == 0 else TH
        for chan, value in enumerate((tre * gim - tim * gre, -(tre * gre + tim * gim))):
            back_ref[chan, :total_rows] = jnp.zeros((total_rows, PIX), F32)
            back_ref[chan, pl.ds(row, PIX), :] = value
            grad_ref[slot, chan] = back_ref[chan, :TH]
            if slot == 0:
                down_ref[chan] = back_ref[chan, TH:]


def spread_kernel(blocks, grad_ref, up_ref, shifts_ref, pos_ref, prev_ref, out_ref, acc_ref):
    angle = lax.axis_index("ang")
    acc_ref[...] = jnp.zeros_like(acc_ref)
    lane = lanes(TH)
    for slot in range(SLOTS + 1):
        if slot < SLOTS:
            col = slot_col(pos_ref, slot, blocks)
        else:
            col = jnp.clip(prev_ref[0, 1], 0, blocks * COLS - PIX)
        for chan in range(2):
            if slot < SLOTS:
                value = grad_ref[slot, chan]
            else:
                value = jnp.concatenate([up_ref[chan], jnp.zeros((TH - PIX, PIX), F32)], axis=0)
            for z in range(LAYERS):
                first, second, offset = place(col, shifts_ref[angle, z], blocks)
                rolled = pltpu.roll(value, offset, 1)
                rows = pl.ds(chan * CHAN_ROWS + z * TH, TH)
                acc_ref[first, rows, :] += jnp.where(lane >= offset, rolled, 0.0)
                acc_ref[second, rows, :] += jnp.where(lane < offset, rolled, 0.0)
    for b in range(blocks):
        out_ref[b] = acc_ref[b].astype(BF16)


CHUNKS = ((0, 144), (144, 128), (272, 144), (416, 128))
FIRST_HALF = (0, 1)
SECOND_HALF = (2, 3)
ALL_CHUNKS = (0, 1, 2, 3)


def ring(blocks):
    me = lax.axis_index("ang")
    right = lax.rem(me + 1, blocks)
    left = lax.rem(me + blocks - 1, blocks)
    return me, right, left


def greet(neighbours):
    barrier = pltpu.get_barrier_semaphore()
    for neighbour in neighbours:
        pl.semaphore_signal(barrier, inc=1, device_id={"ang": neighbour})
    pl.semaphore_wait(barrier, len(neighbours))


def send(src, dst, send_sem, recv_sem, target):
    return pltpu.make_async_remote_copy(
        src_ref=src, dst_ref=dst, send_sem=send_sem, recv_sem=recv_sem, device_id={"ang": target}
    )


def gather_kernel(blocks, delta_ref, beta_ref, out_ref, send_r, recv_r, send_l, recv_l):
    me, right, left = ring(blocks)
    half = blocks // 2
    for chan, ref in enumerate((delta_ref, beta_ref)):
        layers = [ref[pl.ds(z, TH, stride=LAYERS), :] for z in range(LAYERS)]
        rows = pl.ds(chan * CHAN_ROWS, CHAN_ROWS)
        out_ref[me, rows, :] = jnp.concatenate(layers, axis=0).astype(BF16)
    greet((left, right))

    def copy(step, chunk, to_right):
        origin = lax.rem(me - step + blocks, blocks) if to_right else lax.rem(me + step, blocks)
        part = out_ref.at[origin, pl.ds(*CHUNKS[chunk]), :]
        if to_right:
            return send(part, part, send_r.at[step, chunk], recv_r.at[step, chunk], right)
        return send(part, part, send_l.at[step, chunk], recv_l.at[step, chunk], left)

    def arrival(step, chunk, from_left):
        origin = lax.rem(me - step - 1 + blocks, blocks) if from_left else lax.rem(me + step + 1, blocks)
        part = out_ref.at[origin, pl.ds(*CHUNKS[chunk]), :]
        if from_left:
            return send(part, part, send_r.at[step, chunk], recv_r.at[step, chunk], right)
        return send(part, part, send_l.at[step, chunk], recv_l.at[step, chunk], left)

    def carried(step, to_right):
        if step < half - 1:
            return ALL_CHUNKS
        return FIRST_HALF if to_right else SECOND_HALF

    started = []
    for step in range(half):
        for chunk in ALL_CHUNKS:
            for to_right in (True, False):
                if step > 0:
                    arrival(step - 1, chunk, to_right).wait_recv()
                if chunk in carried(step, to_right):
                    item = copy(step, chunk, to_right)
                    item.start()
                    started.append(item)
    for to_right in (True, False):
        for chunk in carried(half - 1, to_right):
            arrival(half - 1, chunk, to_right).wait_recv()
    for item in started:
        item.wait_send()


def reduce_kernel(
    blocks,
    spread_ref,
    delta_ref,
    beta_ref,
    out_r,
    out_l,
    in_r,
    in_l,
    send_r,
    recv_r,
    send_l,
    recv_l,
):
    me, right, left = ring(blocks)
    half = blocks // 2
    greet((left, right))

    def copy(step, chunk, to_right):
        rows = pl.ds(*CHUNKS[chunk])
        if to_right:
            if step == 0:
                src = spread_ref.at[lax.rem(me + half, blocks), rows, :]
            else:
                src = out_r.at[step, rows, :]
            return send(
                src, in_r.at[step, rows, :], send_r.at[step, chunk], recv_r.at[step, chunk], right
            )
        if step == 0:
            src = spread_ref.at[lax.rem(me + half, blocks), rows, :]
        else:
            src = out_l.at[step, rows, :]
        return send(
            src, in_l.at[step, rows, :], send_l.at[step, chunk], recv_l.at[step, chunk], left
        )

    def carried(step, to_right):
        if step > 0:
            return ALL_CHUNKS
        return FIRST_HALF if to_right else SECOND_HALF

    def partial(step, chunk, to_right):
        rows = pl.ds(*CHUNKS[chunk])
        if to_right:
            target = lax.rem(me + half - step, blocks)
        else:
            target = lax.rem(me - half + step + blocks, blocks)
        value = spread_ref[target, rows, :]
        if chunk in carried(step - 1, to_right):
            copy(step - 1, chunk, to_right).wait_recv()
            coming = in_r if to_right else in_l
            value = (value.astype(F32) + coming[step - 1, rows, :].astype(F32)).astype(BF16)
        going = out_r if to_right else out_l
        going[step, rows, :] = value

    started = []
    for step in range(half):
        for chunk in ALL_CHUNKS:
            ways = [way for way in (True, False) if chunk in carried(step, way)]
            if step > 0:
                for way in ways:
                    partial(step, chunk, way)
            for way in ways:
                item = copy(step, chunk, way)
                item.start()
                started.append(item)
    for chunk in ALL_CHUNKS:
        for way in (True, False):
            copy(half - 1, chunk, way).wait_recv()
    for chan, ref in enumerate((delta_ref, beta_ref)):
        rows = pl.ds(chan * CHAN_ROWS, CHAN_ROWS)
        total = in_r[half - 1, rows, :].astype(F32) + in_l[half - 1, rows, :].astype(F32)
        total = total + spread_ref[me, rows, :].astype(F32)
        for z in range(LAYERS):
            ref[pl.ds(z, TH, stride=LAYERS), :] = total[z * TH : (z + 1) * TH]
    for item in started:
        item.wait_send()


VMEM = pl.BlockSpec(memory_space=pltpu.VMEM)
SMEM = pl.BlockSpec(memory_space=pltpu.SMEM)
PARAMS = pltpu.CompilerParams(vmem_limit_bytes=48 << 20)


def comm_params(number):
    return pltpu.CompilerParams(
        vmem_limit_bytes=48 << 20, collective_id=number, has_side_effects=True
    )


def shift_rows(value, steps):
    count = lax.axis_size("rows")
    first, last = max(0, -steps), min(count, count - steps)
    return lax.ppermute(value, "rows", [(i, i + steps) for i in range(first, last)])


def on_device(delta_obj, beta_obj, layer_shifts, field, amplitudes, positions, counts):
    blocks = lax.axis_size("ang")
    m1h, m1l, m2h, m2l = dft_constants()
    prev = shift_rows(positions[0, :1], 1)
    half = blocks // 2
    gathered = pl.pallas_call(
        functools.partial(gather_kernel, blocks),
        out_shape=jax.ShapeDtypeStruct((blocks, BLOCK_ROWS, COLS), BF16),
        in_specs=[VMEM, VMEM],
        out_specs=VMEM,
        scratch_shapes=[pltpu.SemaphoreType.DMA((half, len(CHUNKS)))] * 4,
        compiler_params=comm_params(0),
    )(delta_obj.reshape(CHAN_ROWS, COLS), beta_obj.reshape(CHAN_ROWS, COLS))
    strip = pl.pallas_call(
        functools.partial(halo_kernel, blocks),
        out_shape=jax.ShapeDtypeStruct((2, PIX, PIX), F32),
        in_specs=[VMEM, SMEM, SMEM],
        out_specs=VMEM,
        compiler_params=PARAMS,
    )(gathered, layer_shifts, prev)
    halo = shift_rows(strip, -1)
    grads, down = pl.pallas_call(
        functools.partial(scan_kernel, blocks),
        out_shape=(
            jax.ShapeDtypeStruct((SLOTS, 2, TH, PIX), F32),
            jax.ShapeDtypeStruct((2, PIX, PIX), F32),
        ),
        in_specs=[VMEM] * 8 + [SMEM] * 3,
        out_specs=(VMEM, VMEM),
        scratch_shapes=[
            pltpu.VMEM((SLOTS, 2, TH + PIX, PIX), F32),
            pltpu.VMEM((SLOTS, 2, PIX, PIX), F32),
            pltpu.VMEM((2, TH + PIX, PIX), F32),
        ],
        compiler_params=PARAMS,
    )(gathered, halo, field, amplitudes, m1h, m1l, m2h, m2l, layer_shifts, positions, counts)
    up = shift_rows(down, 1)
    spread = pl.pallas_call(
        functools.partial(spread_kernel, blocks),
        out_shape=jax.ShapeDtypeStruct((blocks, BLOCK_ROWS, COLS), BF16),
        in_specs=[VMEM, VMEM, SMEM, SMEM, SMEM],
        out_specs=VMEM,
        scratch_shapes=[pltpu.VMEM((blocks, BLOCK_ROWS, COLS), F32)],
        compiler_params=PARAMS,
    )(grads, up, layer_shifts, positions, prev)
    grad = jax.ShapeDtypeStruct((CHAN_ROWS, COLS), F32)
    delta_grad, beta_grad = pl.pallas_call(
        functools.partial(reduce_kernel, blocks),
        out_shape=(grad, grad),
        in_specs=[VMEM],
        out_specs=(VMEM, VMEM),
        scratch_shapes=[pltpu.VMEM((half, BLOCK_ROWS, COLS), BF16)] * 4
        + [pltpu.SemaphoreType.DMA((half, len(CHUNKS)))] * 4,
        compiler_params=comm_params(1),
    )(spread)
    shape = (TH, LAYERS, COLS)
    return (delta_grad.reshape(shape), beta_grad.reshape(shape))


def solution(mesh):
    placed = (
        P("rows", None, "ang"),
        P("rows", None, "ang"),
        P(),
        P(),
        P("ang", "rows", None, None),
        P("ang", "rows", None),
        P("ang", "rows"),
    )
    return jax.shard_map(
        on_device,
        mesh=mesh,
        in_specs=placed,
        out_specs=(P("rows", None, "ang"), P("rows", None, "ang")),
        check_vma=False,
    )
```

```python
import functools
import math

import jax
import jax.numpy as jnp
import numpy as np
from jax import lax
from jax.experimental import pallas as pl
from jax.experimental.pallas import tpu as pltpu
from jax.sharding import PartitionSpec as P

PIX = 128
TH = 136
COLS = 128
LAYERS = 2
SHIFT = 8
SLOTS = 4
AMP_FLOOR = 0.1
BLOCK_ROWS = 2 * LAYERS * TH
CHAN_ROWS = LAYERS * TH
F32 = jnp.float32
BF16 = jnp.bfloat16


def dft_constants():
    counter = np.arange(PIX)
    angle = (counter[:, None] * counter[None, :] % PIX) * (2.0 * math.pi / PIX)
    scale = 1.0 / math.sqrt(PIX)
    re = np.cos(angle) * scale
    im = -np.sin(angle) * scale
    m1 = np.block([[re, -im], [im, re]])
    m2 = np.block([[re, im], [-im, re]])

    def split(m):
        hi = m.astype(BF16)
        lo = (m - hi.astype(np.float64)).astype(BF16)
        return np.asarray(hi), np.asarray(lo)

    return split(m1) + split(m2)


def split_f32(x):
    hi = x.astype(BF16)
    lo = (x - hi.astype(F32)).astype(BF16)
    return hi, lo


def dot(a, b):
    return jnp.dot(a, b, preferred_element_type=F32)


def left_product(hi, lo, data):
    d_hi, d_lo = split_f32(data)
    return dot(hi, d_hi) + (dot(hi, d_lo) + dot(lo, d_hi))


def right_product(data, hi, lo):
    d_hi, d_lo = split_f32(data)
    return dot(d_hi, hi) + (dot(d_lo, hi) + dot(d_hi, lo))


def sin_cos(x):
    k = jnp.floor(x * (2.0 / math.pi) + 0.5)
    y = x - k * 1.5703125
    y = y - k * 4.837512969970703125e-4
    y = y - k * 7.54978995489188216e-8
    q = k.astype(jnp.int32)
    y2 = y * y
    s = y + y * y2 * (-1.6666654611e-1 + y2 * (8.3321608736e-3 + y2 * -1.9515295891e-4))
    c = (1.0 - 0.5 * y2) + y2 * y2 * (
        4.166664568298827e-2 + y2 * (-1.388731625493765e-3 + y2 * 2.443315711809948e-5)
    )
    odd = (q & 1) == 1
    sn = jnp.where(odd, c, s)
    cs = jnp.where(odd, s, c)
    sn = jnp.where((q & 2) == 2, -sn, sn)
    cs = jnp.where(((q + 1) & 2) == 2, -cs, cs)
    return sn, cs


def place(col, shift, blocks):
    start = col + shift
    start = jnp.where(start < 0, start + blocks * COLS, start)
    first = jnp.right_shift(start, 7)
    offset = start & (COLS - 1)
    second = jnp.where(first == blocks - 1, 0, first + 1)
    return first, second, offset


CHUNKS = ((0, 144), (144, 128), (272, 144), (416, 128))
FIRST_HALF = (0, 1)
SECOND_HALF = (2, 3)
ALL_CHUNKS = (0, 1, 2, 3)
STRIPS = SLOTS + 1
PREV = SLOTS


def kernel(
    blocks,
    tiles,
    delta_hbm,
    beta_hbm,
    field_hbm,
    amp_hbm,
    m1h_hbm,
    m1l_hbm,
    m2h_hbm,
    m2l_hbm,
    shifts_ref,
    pos_ref,
    count_ref,
    pos_hbm,
    delta_out,
    beta_out,
    object_ref,
    field_ref,
    amp_ref,
    m1h_ref,
    m1l_ref,
    m2h_ref,
    m2l_ref,
    prev_pos_vmem,
    prev_pos,
    g_ref,
    strip_ref,
    strip_own,
    strip_prev,
    trans_ref,
    back_ref,
    rolled_ref,
    out_r,
    out_l,
    in_r,
    in_l,
    load_sem,
    edge_send,
    edge_recv,
    send_r,
    recv_r,
    send_l,
    recv_l,
    send_r2,
    recv_r2,
    send_l2,
    recv_l2,
):
    me = lax.axis_index("ang")
    right = lax.rem(me + 1, blocks)
    left = lax.rem(me + blocks - 1, blocks)
    tile = lax.axis_index("rows")
    below = lax.rem(tile + 1, tiles)
    above = lax.rem(tile + tiles - 1, tiles)
    half = blocks // 2

    loads = [
        pltpu.make_async_copy(src, dst, load_sem.at[i])
        for i, (src, dst) in enumerate(
            (
                (delta_hbm, object_ref.at[0]),
                (beta_hbm, object_ref.at[1]),
                (amp_hbm.at[0], amp_ref.at[pl.ds(0, SLOTS)]),
                (field_hbm, field_ref),
                (m1h_hbm, m1h_ref),
                (m1l_hbm, m1l_ref),
                (m2h_hbm, m2h_ref),
                (m2l_hbm, m2l_ref),
            )
        )
    ]
    for item in loads:
        item.start()
    barrier = pltpu.get_barrier_semaphore()
    for target in ({"ang": left}, {"ang": right}, {"rows": above}, {"rows": below}):
        pl.semaphore_signal(barrier, inc=1, device_id=target)
    for chan in range(2):
        loads[chan].wait()
        layers = [object_ref[chan, pl.ds(z, TH, stride=LAYERS), :] for z in range(LAYERS)]
        rows = pl.ds(chan * CHAN_ROWS, CHAN_ROWS)
        g_ref[me, rows, :] = jnp.concatenate(layers, axis=0).astype(BF16)
    pl.semaphore_wait(barrier, 4)

    def remote(src, dst, send_sem, recv_sem, target):
        return pltpu.make_async_remote_copy(
            src_ref=src, dst_ref=dst, send_sem=send_sem, recv_sem=recv_sem, device_id=target
        )

    def edge(index, src, dst, target):
        return remote(src, dst, edge_send.at[index], edge_recv.at[index], target)

    def gather_copy(step, chunk, to_right, coming=False):
        hops = step + 1 if coming else step
        if to_right:
            origin = lax.rem(me - hops + blocks, blocks)
        else:
            origin = lax.rem(me + hops, blocks)
        part = g_ref.at[origin, pl.ds(*CHUNKS[chunk]), :]
        if to_right:
            return remote(
                part, part, send_r.at[step, chunk], recv_r.at[step, chunk], {"ang": right}
            )
        return remote(part, part, send_l.at[step, chunk], recv_l.at[step, chunk], {"ang": left})

    def gathered(step, to_right):
        if step < half - 1:
            return ALL_CHUNKS
        return FIRST_HALF if to_right else SECOND_HALF

    pos_edge = edge(0, pos_hbm.at[0], prev_pos_vmem, {"rows": below})
    amp_edge = edge(1, amp_hbm.at[0, 0], amp_ref.at[PREV], {"rows": below})
    started = [pos_edge, amp_edge]
    for step in range(half):
        for index in range(len(ALL_CHUNKS)):
            for to_right in (True, False):
                chunk = ALL_CHUNKS[index if to_right else -1 - index]
                if step > 0:
                    gather_copy(step - 1, chunk, to_right, coming=True).wait_recv()
                if chunk in gathered(step, to_right):
                    item = gather_copy(step, chunk, to_right)
                    item.start()
                    started.append(item)
        if step == 0:
            pos_edge.start()
            amp_edge.start()
        if step == 3:
            pos_edge.wait_recv()
            prev_load = pltpu.make_async_copy(prev_pos_vmem, prev_pos, load_sem.at[8])
            prev_load.start()
    for item in loads[2:]:
        item.wait()
    prev_load.wait()
    amp_edge.wait_recv()
    for to_right in (True, False):
        for chunk in gathered(half - 1, to_right):
            gather_copy(half - 1, chunk, to_right, coming=True).wait_recv()

    lane = lax.broadcasted_iota(jnp.int32, (TH, COLS), 1)
    cols, firsts, seconds, offsets, row_starts = [], [], [], [], []
    for slot in range(STRIPS):
        row = prev_pos[0, 0] if slot == PREV else pos_ref[0, 0, slot]
        col = prev_pos[1, 0] if slot == PREV else pos_ref[0, 1, slot]
        row_starts.append(jnp.clip(row, 0, TH if slot in (0, PREV) else TH - PIX))
        cols.append(jnp.clip(col, 0, blocks * COLS - PIX))
        spots = [place(cols[slot], shifts_ref[z, me], blocks) for z in range(LAYERS)]
        firsts.append([spot[0] for spot in spots])
        seconds.append([spot[1] for spot in spots])
        offsets.append([spot[2] for spot in spots])

    def strip(slot, chan):
        total = None
        for z in range(LAYERS):
            rows = pl.ds(chan * CHAN_ROWS, CHAN_ROWS)
            offset = offsets[slot][z]
            part0 = g_ref[firsts[slot][z], rows, :].astype(F32)[z * TH : (z + 1) * TH]
            part1 = g_ref[seconds[slot][z], rows, :].astype(F32)[z * TH : (z + 1) * TH]
            both = jnp.where(lane >= offset, part0, part1)
            value = pltpu.roll(both, (COLS - offset) & (COLS - 1), 1)
            total = value if total is None else total + value
        return total

    for chan in range(2):
        strip_prev[chan, TH:] = strip(PREV, chan)
        strip_prev[chan, :SHIFT] = jnp.zeros((SHIFT, COLS), F32)
        strip_own[chan, :TH] = strip(0, chan)
    lower = pl.ds(TH, PIX)
    upper = pl.ds(SHIFT, PIX)
    up_edge = edge(2, strip_prev.at[:, lower, :], strip_own.at[:, lower, :], {"rows": above})
    down_edge = edge(3, strip_own.at[:, upper, :], strip_prev.at[:, upper, :], {"rows": below})
    for item in (up_edge, down_edge):
        item.start()
        started.append(item)
    for slot in range(1, SLOTS):
        for chan in range(2):
            strip_ref[slot - 1, chan] = strip(slot, chan)

    probe_re = field_ref[0]
    probe_im = field_ref[1]
    depth = lax.broadcasted_iota(jnp.int32, (PIX, PIX), 0)

    def patch(slot, chan):
        rows = pl.ds(row_starts[slot], PIX)
        if slot == PREV:
            return strip_prev[chan, rows, :]
        if slot > 0:
            return strip_ref[slot - 1, chan, rows, :]
        value = strip_own[chan, rows, :]
        outside = (depth + row_starts[slot] >= TH) & (tile == tiles - 1)
        return jnp.where(outside, 0.0, value)

    def scans(slots):
        number = len(slots)
        exit_re, exit_im = [], []
        for slot in slots:
            damping = jnp.exp(-patch(slot, 1))
            sn, cs = sin_cos(patch(slot, 0))
            tre = damping * cs
            tim = damping * sn
            trans_ref[slot, 0] = tre
            trans_ref[slot, 1] = tim
            exit_re.append(probe_re * tre - probe_im * tim)
            exit_im.append(probe_re * tim + probe_im * tre)
        data = jnp.concatenate(
            [jnp.concatenate(exit_re, axis=1), jnp.concatenate(exit_im, axis=1)], axis=0
        )
        wide = left_product(m1h_ref[...], m1l_ref[...], data)
        wide = jnp.concatenate(
            [
                jnp.concatenate(
                    [wide[:PIX, j * PIX : (j + 1) * PIX], wide[PIX:, j * PIX : (j + 1) * PIX]],
                    axis=1,
                )
                for j in range(number)
            ],
            axis=0,
        )
        far = right_product(wide, m2h_ref[...], m2l_ref[...])
        residual = []
        for j, slot in enumerate(slots):
            rows = far[j * PIX : (j + 1) * PIX]
            re, im = rows[:, :PIX], rows[:, PIX:]
            live = tile > 0 if slot == PREV else slot < count_ref[0, 0]
            inverse = lax.rsqrt(jnp.maximum(re * re + im * im, AMP_FLOOR * AMP_FLOOR))
            factor = jnp.where(live, 1.0 - amp_ref[slot] * inverse, 0.0)
            residual.append(jnp.concatenate([re * factor, im * factor], axis=1))
        back = right_product(jnp.concatenate(residual, axis=0), m1h_ref[...], m1l_ref[...])
        tall = jnp.concatenate(
            [
                jnp.concatenate([back[j * PIX : (j + 1) * PIX, :PIX] for j in range(number)], axis=1),
                jnp.concatenate([back[j * PIX : (j + 1) * PIX, PIX:] for j in range(number)], axis=1),
            ],
            axis=0,
        )
        grad = left_product(m2h_ref[...], m2l_ref[...], tall)
        for j, slot in enumerate(slots):
            bre = grad[:PIX, j * PIX : (j + 1) * PIX]
            bim = grad[PIX:, j * PIX : (j + 1) * PIX]
            gre = probe_re * bre + probe_im * bim
            gim = probe_re * bim - probe_im * bre
            tre = trans_ref[slot, 0]
            tim = trans_ref[slot, 1]
            at = TH if slot == 0 else 0 if slot == PREV else SHIFT
            bottom = SHIFT if slot != PREV else TH + SHIFT
            start = (SHIFT if slot in range(1, SLOTS) else TH) - row_starts[slot]
            for chan, value in enumerate((tre * gim - tim * gre, -(tre * gre + tim * gim))):
                if at:
                    back_ref[slot, chan, :at] = jnp.zeros((at, PIX), F32)
                back_ref[slot, chan, at : at + PIX] = value
                back_ref[slot, chan, at + PIX : at + PIX + bottom] = jnp.zeros((bottom, PIX), F32)
                placed = back_ref[slot, chan, pl.ds(start, TH), :]
                for z in range(LAYERS):
                    first_row = chan * CHAN_ROWS + z * TH
                    rolled_ref[slot, first_row : first_row + TH] = pltpu.roll(
                        placed, offsets[slot][z], 1
                    )

    scans((1, 2, 3))
    up_edge.wait_recv()
    down_edge.wait_recv()
    scans((0, PREV))

    line = lax.broadcasted_iota(jnp.int32, (8, COLS), 1)

    def contribution(target, chunk):
        begin, size = CHUNKS[chunk]
        pieces = []
        for z_start in range(0, BLOCK_ROWS, TH):
            low, high = max(begin, z_start), min(begin + size, z_start + TH)
            if low >= high:
                continue
            z = (z_start // TH) % LAYERS
            total = None
            for slot in range(STRIPS):
                offset = offsets[slot][z]
                in_first = target == firsts[slot][z]
                in_second = target == seconds[slot][z]
                least = jnp.where(in_first, offset, jnp.where(in_second, 0, COLS))
                most = jnp.where(in_first, COLS, jnp.where(in_second, offset, 0))
                inside = (lane[: high - low] >= least) & (lane[: high - low] < most)
                value = jnp.where(inside, rolled_ref[slot, low:high], 0.0)
                total = value if total is None else total + value
            pieces.append(total)
        return jnp.concatenate(pieces, axis=0) if len(pieces) > 1 else pieces[0]

    def reduce_copy(step, chunk, to_right):
        rows = pl.ds(*CHUNKS[chunk])
        if to_right:
            return remote(
                out_r.at[step, rows, :],
                in_r.at[step, rows, :],
                send_r2.at[step, chunk],
                recv_r2.at[step, chunk],
                {"ang": right},
            )
        return remote(
            out_l.at[step, rows, :],
            in_l.at[step, rows, :],
            send_l2.at[step, chunk],
            recv_l2.at[step, chunk],
            {"ang": left},
        )

    def reduced(step, to_right):
        if step > 0:
            return ALL_CHUNKS
        return FIRST_HALF if to_right else SECOND_HALF

    def partial(step, chunk, to_right):
        rows = pl.ds(*CHUNKS[chunk])
        if to_right:
            target = lax.rem(me + half - step, blocks)
        else:
            target = lax.rem(me - half + step + blocks, blocks)
        value = contribution(target, chunk).astype(BF16)
        if step > 0 and chunk in reduced(step - 1, to_right):
            reduce_copy(step - 1, chunk, to_right).wait_recv()
            coming = in_r if to_right else in_l
            value = (value.astype(F32) + coming[step - 1, rows, :].astype(F32)).astype(BF16)
        going = out_r if to_right else out_l
        going[step, rows, :] = value

    for step in range(half):
        for index in range(len(ALL_CHUNKS)):
            ways = []
            for to_right in (True, False):
                chunk = ALL_CHUNKS[index if to_right else -1 - index]
                if chunk in reduced(step, to_right):
                    partial(step, chunk, to_right)
                    ways.append((chunk, to_right))
            for chunk, to_right in ways:
                item = reduce_copy(step, chunk, to_right)
                item.start()
                started.append(item)
    own = [
        contribution(me, chunk).astype(BF16).astype(F32) for chunk in ALL_CHUNKS
    ]
    for chunk in ALL_CHUNKS:
        for to_right in (True, False):
            reduce_copy(half - 1, chunk, to_right).wait_recv()
    own = jnp.concatenate(own, axis=0)
    for chan, ref in enumerate((delta_out, beta_out)):
        rows = pl.ds(chan * CHAN_ROWS, CHAN_ROWS)
        total = in_r[half - 1, rows, :].astype(F32) + in_l[half - 1, rows, :].astype(F32)
        total = total + own[chan * CHAN_ROWS : (chan + 1) * CHAN_ROWS]
        for z in range(LAYERS):
            ref[pl.ds(z, TH, stride=LAYERS), :] = total[z * TH : (z + 1) * TH]
    for item in started:
        item.wait_send()


VMEM = pl.BlockSpec(memory_space=pltpu.VMEM)
SMEM = pl.BlockSpec(memory_space=pltpu.SMEM)
HBM = pl.BlockSpec(memory_space=pltpu.HBM)


def on_device(delta_obj, beta_obj, layer_shifts, field, amplitudes, positions, counts):
    blocks = lax.axis_size("ang")
    tiles = lax.axis_size("rows")
    half = blocks // 2
    table = pltpu.VMEM((2 * PIX, 2 * PIX), BF16)
    stage = pltpu.VMEM((half, BLOCK_ROWS, COLS), BF16)
    ring_sems = pltpu.SemaphoreType.DMA((half, len(CHUNKS)))
    grad = jax.ShapeDtypeStruct((CHAN_ROWS, COLS), F32)
    pos = jnp.swapaxes(positions, 1, 2)
    delta_grad, beta_grad = pl.pallas_call(
        functools.partial(kernel, blocks, tiles),
        out_shape=(grad, grad),
        in_specs=[HBM] * 8 + [SMEM] * 3 + [HBM],
        out_specs=(VMEM, VMEM),
        scratch_shapes=[
            pltpu.VMEM((2, CHAN_ROWS, COLS), F32),
            pltpu.VMEM((2, PIX, PIX), F32),
            pltpu.VMEM((STRIPS, PIX, PIX), F32),
            table,
            table,
            table,
            table,
            pltpu.VMEM((2, SLOTS), jnp.int32),
            pltpu.SMEM((2, SLOTS), jnp.int32),
            pltpu.VMEM((blocks, BLOCK_ROWS, COLS), BF16),
            pltpu.VMEM((SLOTS - 1, 2, TH, PIX), F32),
            pltpu.VMEM((2, 2 * TH, PIX), F32),
            pltpu.VMEM((2, 2 * TH, PIX), F32),
            pltpu.VMEM((STRIPS, 2, PIX, PIX), F32),
            pltpu.VMEM((STRIPS, 2, 2 * TH, PIX), F32),
            pltpu.VMEM((STRIPS, BLOCK_ROWS, COLS), F32),
            stage,
            stage,
            stage,
            stage,
            pltpu.SemaphoreType.DMA((9,)),
            pltpu.SemaphoreType.DMA((4,)),
            pltpu.SemaphoreType.DMA((4,)),
        ]
        + [ring_sems] * 8,
        compiler_params=pltpu.CompilerParams(
            vmem_limit_bytes=67043328, collective_id=0, has_side_effects=True
        ),
    )(
        delta_obj.reshape(CHAN_ROWS, COLS),
        beta_obj.reshape(CHAN_ROWS, COLS),
        field,
        amplitudes,
        *dft_constants(),
        layer_shifts.T,
        pos,
        counts,
        pos,
    )
    shape = (TH, LAYERS, COLS)
    return (delta_grad.reshape(shape), beta_grad.reshape(shape))


def solution(mesh):
    placed = (
        P("rows", None, "ang"),
        P("rows", None, "ang"),
        P(),
        P(),
        P("ang", "rows", None, None),
        P("ang", "rows", None),
        P("ang", "rows"),
    )
    return jax.shard_map(
        on_device,
        mesh=mesh,
        in_specs=placed,
        out_specs=(P("rows", None, "ang"), P("rows", None, "ang")),
        check_vma=False,
    )
```

```python
import functools
import math

import jax
import jax.numpy as jnp
import numpy as np
from jax import lax
from jax.experimental import pallas as pl
from jax.experimental.pallas import tpu as pltpu
from jax.sharding import PartitionSpec as P

PIX = 128
TH = 136
COLS = 128
LAYERS = 2
SHIFT = 8
SLOTS = 4
AMP_FLOOR = 0.1
BLOCK_ROWS = 2 * LAYERS * TH
CHAN_ROWS = LAYERS * TH
F32 = jnp.float32
BF16 = jnp.bfloat16


def dft_constants():
    counter = np.arange(PIX)
    angle = (counter[:, None] * counter[None, :] % PIX) * (2.0 * math.pi / PIX)
    scale = 1.0 / math.sqrt(PIX)
    re = np.cos(angle) * scale
    im = -np.sin(angle) * scale
    m1 = np.block([[re, -im], [im, re]])
    m2 = np.block([[re, im], [-im, re]])

    def split(m):
        hi = m.astype(BF16)
        lo = (m - hi.astype(np.float64)).astype(BF16)
        return np.asarray(hi), np.asarray(lo)

    return split(m1) + split(m2)


def split_f32(x):
    hi = x.astype(BF16)
    lo = (x - hi.astype(F32)).astype(BF16)
    return hi, lo


def dot(a, b):
    return jnp.dot(a, b, preferred_element_type=F32)


def left_product(hi, lo, data):
    d_hi, d_lo = split_f32(data)
    return dot(hi, d_hi) + (dot(hi, d_lo) + dot(lo, d_hi))


def right_product(data, hi, lo):
    d_hi, d_lo = split_f32(data)
    return dot(d_hi, hi) + (dot(d_lo, hi) + dot(d_hi, lo))


def sin_cos(x):
    k = jnp.floor(x * (2.0 / math.pi) + 0.5)
    y = x - k * 1.5703125
    y = y - k * 4.837512969970703125e-4
    y = y - k * 7.54978995489188216e-8
    q = k.astype(jnp.int32)
    y2 = y * y
    s = y + y * y2 * (-1.6666654611e-1 + y2 * (8.3321608736e-3 + y2 * -1.9515295891e-4))
    c = (1.0 - 0.5 * y2) + y2 * y2 * (
        4.166664568298827e-2 + y2 * (-1.388731625493765e-3 + y2 * 2.443315711809948e-5)
    )
    odd = (q & 1) == 1
    sn = jnp.where(odd, c, s)
    cs = jnp.where(odd, s, c)
    sn = jnp.where((q & 2) == 2, -sn, sn)
    cs = jnp.where(((q + 1) & 2) == 2, -cs, cs)
    return sn, cs


def place(col, shift, blocks):
    start = col + shift
    start = jnp.where(start < 0, start + blocks * COLS, start)
    first = jnp.right_shift(start, 7)
    offset = start & (COLS - 1)
    second = jnp.where(first == blocks - 1, 0, first + 1)
    return first, second, offset


PARTS = (144, 128)


def chunk_table():
    table, start = [], 0
    for size in PARTS * 2:
        table.append((start, size))
        start += size
    return tuple(table)


CHUNKS = chunk_table()
ALL_CHUNKS = tuple(range(len(CHUNKS)))
FIRST_HALF = ALL_CHUNKS[: len(PARTS)]
SECOND_HALF = ALL_CHUNKS[len(PARTS) :]
STRIPS = SLOTS + 1
PREV = SLOTS


def kernel(
    blocks,
    tiles,
    delta_hbm,
    beta_hbm,
    field_hbm,
    amp_hbm,
    m1h_hbm,
    m1l_hbm,
    m2h_hbm,
    m2l_hbm,
    shifts_hbm,
    pos_hbm,
    count_hbm,
    out_ref,
    object_ref,
    field_ref,
    amp_ref,
    m1h_ref,
    m1l_ref,
    m2h_ref,
    m2l_ref,
    shifts_ref,
    pos_ref,
    count_ref,
    prev_pos_vmem,
    prev_pos,
    g_ref,
    strip_ref,
    strip_own,
    strip_prev,
    trans_ref,
    back_ref,
    rolled_ref,
    out_r,
    out_l,
    in_r,
    in_l,
    load_sem,
    edge_send,
    edge_recv,
    send_r,
    recv_r,
    send_l,
    recv_l,
    send_r2,
    recv_r2,
    send_l2,
    recv_l2,
    ready_ref,
):
    me = lax.axis_index("ang")
    right = lax.rem(me + 1, blocks)
    left = lax.rem(me + blocks - 1, blocks)
    tile = lax.axis_index("rows")
    below = lax.rem(tile + 1, tiles)
    above = lax.rem(tile + tiles - 1, tiles)
    half = blocks // 2

    loads = [
        pltpu.make_async_copy(src, dst, load_sem.at[i])
        for i, (src, dst) in enumerate(
            (
                (delta_hbm, object_ref.at[0]),
                (beta_hbm, object_ref.at[1]),
                (amp_hbm.at[0], amp_ref.at[pl.ds(0, SLOTS)]),
                (field_hbm, field_ref),
                (m1h_hbm, m1h_ref),
                (m1l_hbm, m1l_ref),
                (m2h_hbm, m2h_ref),
                (m2l_hbm, m2l_ref),
                (shifts_hbm, shifts_ref),
                (pos_hbm, pos_ref),
                (count_hbm, count_ref),
            )
        )
    ]
    for item in loads:
        item.start()
    barrier = pltpu.get_barrier_semaphore()
    for target in ({"ang": left}, {"ang": right}, {"rows": above}, {"rows": below}):
        pl.semaphore_signal(barrier, inc=1, device_id=target)
    for chan in range(2):
        loads[chan].wait()
        layers = [object_ref[chan, pl.ds(z, TH, stride=LAYERS), :] for z in range(LAYERS)]
        rows = pl.ds(chan * CHAN_ROWS, CHAN_ROWS)
        g_ref[me, rows, :] = jnp.concatenate(layers, axis=0).astype(BF16)
    pl.semaphore_wait(barrier, 4)

    def remote(src, dst, send_sem, recv_sem, target):
        return pltpu.make_async_remote_copy(
            src_ref=src, dst_ref=dst, send_sem=send_sem, recv_sem=recv_sem, device_id=target
        )

    def edge(index, src, dst, target):
        return remote(src, dst, edge_send.at[index], edge_recv.at[index], target)

    def gather_copy(step, chunk, to_right, coming=False):
        hops = step + 1 if coming else step
        if to_right:
            origin = lax.rem(me - hops + blocks, blocks)
        else:
            origin = lax.rem(me + hops, blocks)
        part = g_ref.at[origin, pl.ds(*CHUNKS[chunk]), :]
        if to_right:
            return remote(
                part, part, send_r.at[step, chunk], recv_r.at[step, chunk], {"ang": right}
            )
        return remote(part, part, send_l.at[step, chunk], recv_l.at[step, chunk], {"ang": left})

    def gathered(step, to_right):
        if step < half - 1:
            return ALL_CHUNKS
        return FIRST_HALF if to_right else SECOND_HALF

    pos_edge = edge(0, pos_hbm.at[0], prev_pos_vmem, {"rows": below})
    amp_edge = edge(1, amp_hbm.at[0, 0], amp_ref.at[PREV], {"rows": below})
    started = [pos_edge, amp_edge]
    for step in range(half):
        for index in range(len(ALL_CHUNKS)):
            for to_right in (True, False):
                chunk = ALL_CHUNKS[index if to_right else -1 - index]
                if step > 0:
                    gather_copy(step - 1, chunk, to_right, coming=True).wait_recv()
                if chunk in gathered(step, to_right):
                    item = gather_copy(step, chunk, to_right)
                    item.start()
                    started.append(item)
        if step == 0:
            pos_edge.start()
            amp_edge.start()
        if step == 3:
            pos_edge.wait_recv()
            prev_load = pltpu.make_async_copy(prev_pos_vmem, prev_pos, load_sem.at[11])
            prev_load.start()
    for item in loads[2:]:
        item.wait()
    prev_load.wait()
    amp_edge.wait_recv()
    for to_right in (True, False):
        for chunk in gathered(half - 1, to_right):
            gather_copy(half - 1, chunk, to_right, coming=True).wait_recv()

    lane = lax.broadcasted_iota(jnp.int32, (TH, COLS), 1)
    cols, firsts, seconds, offsets, row_starts = [], [], [], [], []
    for slot in range(STRIPS):
        row = prev_pos[0, 0] if slot == PREV else pos_ref[0, 0, slot]
        col = prev_pos[1, 0] if slot == PREV else pos_ref[0, 1, slot]
        row_starts.append(jnp.clip(row, 0, TH if slot in (0, PREV) else TH - PIX))
        cols.append(jnp.clip(col, 0, blocks * COLS - PIX))
        spots = [place(cols[slot], shifts_ref[z, me], blocks) for z in range(LAYERS)]
        firsts.append([spot[0] for spot in spots])
        seconds.append([spot[1] for spot in spots])
        offsets.append([spot[2] for spot in spots])

    def strip(slot, chan):
        total = None
        for z in range(LAYERS):
            rows = pl.ds(chan * CHAN_ROWS, CHAN_ROWS)
            offset = offsets[slot][z]
            part0 = g_ref[firsts[slot][z], rows, :].astype(F32)[z * TH : (z + 1) * TH]
            part1 = g_ref[seconds[slot][z], rows, :].astype(F32)[z * TH : (z + 1) * TH]
            both = jnp.where(lane >= offset, part0, part1)
            value = pltpu.roll(both, (COLS - offset) & (COLS - 1), 1)
            total = value if total is None else total + value
        return total

    lower = pl.ds(TH, PIX)
    upper = pl.ds(SHIFT, PIX)
    strip_edges = []
    for chan in range(2):
        strip_prev[chan, TH:] = strip(PREV, chan)
        strip_prev[chan, :SHIFT] = jnp.zeros((SHIFT, COLS), F32)
        strip_own[chan, :TH] = strip(0, chan)
        strip_edges += [
            edge(
                2 + chan, strip_prev.at[chan, lower, :], strip_own.at[chan, lower, :], {"rows": above}
            ),
            edge(
                4 + chan, strip_own.at[chan, upper, :], strip_prev.at[chan, upper, :], {"rows": below}
            ),
        ]
        for item in strip_edges[-2:]:
            item.start()
    started += strip_edges
    for slot in range(1, SLOTS):
        for chan in range(2):
            strip_ref[slot - 1, chan] = strip(slot, chan)

    probe_re = field_ref[0]
    probe_im = field_ref[1]
    depth = lax.broadcasted_iota(jnp.int32, (PIX, PIX), 0)

    def patch(slot, chan):
        rows = pl.ds(row_starts[slot], PIX)
        if slot == PREV:
            return strip_prev[chan, rows, :]
        if slot > 0:
            return strip_ref[slot - 1, chan, rows, :]
        value = strip_own[chan, rows, :]
        outside = (depth + row_starts[slot] >= TH) & (tile == tiles - 1)
        return jnp.where(outside, 0.0, value)

    def scans(slots):
        number = len(slots)
        exit_re, exit_im = [], []
        for slot in slots:
            damping = jnp.exp(-patch(slot, 1))
            sn, cs = sin_cos(patch(slot, 0))
            tre = damping * cs
            tim = damping * sn
            trans_ref[slot, 0] = tre
            trans_ref[slot, 1] = tim
            exit_re.append(probe_re * tre - probe_im * tim)
            exit_im.append(probe_re * tim + probe_im * tre)
        data = jnp.concatenate(
            [jnp.concatenate(exit_re, axis=1), jnp.concatenate(exit_im, axis=1)], axis=0
        )
        wide = left_product(m1h_ref[...], m1l_ref[...], data)
        wide = jnp.concatenate(
            [
                jnp.concatenate(
                    [wide[:PIX, j * PIX : (j + 1) * PIX], wide[PIX:, j * PIX : (j + 1) * PIX]],
                    axis=1,
                )
                for j in range(number)
            ],
            axis=0,
        )
        far = right_product(wide, m2h_ref[...], m2l_ref[...])
        residual = []
        for j, slot in enumerate(slots):
            rows = far[j * PIX : (j + 1) * PIX]
            re, im = rows[:, :PIX], rows[:, PIX:]
            live = tile > 0 if slot == PREV else slot < count_ref[0, 0]
            inverse = lax.rsqrt(jnp.maximum(re * re + im * im, AMP_FLOOR * AMP_FLOOR))
            factor = jnp.where(live, 1.0 - amp_ref[slot] * inverse, 0.0)
            residual.append(jnp.concatenate([re * factor, im * factor], axis=1))
        back = right_product(jnp.concatenate(residual, axis=0), m1h_ref[...], m1l_ref[...])
        tall = jnp.concatenate(
            [
                jnp.concatenate([back[j * PIX : (j + 1) * PIX, :PIX] for j in range(number)], axis=1),
                jnp.concatenate([back[j * PIX : (j + 1) * PIX, PIX:] for j in range(number)], axis=1),
            ],
            axis=0,
        )
        grad = left_product(m2h_ref[...], m2l_ref[...], tall)
        for j, slot in enumerate(slots):
            bre = grad[:PIX, j * PIX : (j + 1) * PIX]
            bim = grad[PIX:, j * PIX : (j + 1) * PIX]
            gre = probe_re * bre + probe_im * bim
            gim = probe_re * bim - probe_im * bre
            tre = trans_ref[slot, 0]
            tim = trans_ref[slot, 1]
            at = TH if slot == 0 else 0 if slot == PREV else SHIFT
            bottom = SHIFT if slot != PREV else TH + SHIFT
            start = (SHIFT if slot in range(1, SLOTS) else TH) - row_starts[slot]
            for chan, value in enumerate((tre * gim - tim * gre, -(tre * gre + tim * gim))):
                if at:
                    back_ref[slot, chan, :at] = jnp.zeros((at, PIX), F32)
                back_ref[slot, chan, at : at + PIX] = value
                back_ref[slot, chan, at + PIX : at + PIX + bottom] = jnp.zeros((bottom, PIX), F32)
                placed = back_ref[slot, chan, pl.ds(start, TH), :]
                for z in range(LAYERS):
                    first_row = chan * CHAN_ROWS + z * TH
                    rolled_ref[slot, first_row : first_row + TH] = pltpu.roll(
                        placed, offsets[slot][z], 1
                    )

    scans((1, 2, 3))
    for item in strip_edges:
        item.wait_recv()
    scans((0, PREV))

    line = lax.broadcasted_iota(jnp.int32, (8, COLS), 1)

    def contribution(target, chunk):
        begin, size = CHUNKS[chunk]
        pieces = []
        for z_start in range(0, BLOCK_ROWS, TH):
            low, high = max(begin, z_start), min(begin + size, z_start + TH)
            if low >= high:
                continue
            z = (z_start // TH) % LAYERS
            total = None
            for slot in range(STRIPS):
                offset = offsets[slot][z]
                in_first = target == firsts[slot][z]
                in_second = target == seconds[slot][z]
                least = jnp.where(in_first, offset, jnp.where(in_second, 0, COLS))
                most = jnp.where(in_first, COLS, jnp.where(in_second, offset, 0))
                inside = (lane[: high - low] >= least) & (lane[: high - low] < most)
                value = jnp.where(inside, rolled_ref[slot, low:high], 0.0)
                total = value if total is None else total + value
            pieces.append(total)
        return jnp.concatenate(pieces, axis=0) if len(pieces) > 1 else pieces[0]

    def reduce_copy(step, chunk, to_right):
        rows = pl.ds(*CHUNKS[chunk])
        if to_right:
            return remote(
                out_r.at[step, rows, :],
                in_r.at[step, rows, :],
                send_r2.at[step, chunk],
                recv_r2.at[step, chunk],
                {"ang": right},
            )
        return remote(
            out_l.at[step, rows, :],
            in_l.at[step, rows, :],
            send_l2.at[step, chunk],
            recv_l2.at[step, chunk],
            {"ang": left},
        )

    def reduced(step, to_right):
        if step > 0:
            return ALL_CHUNKS
        return FIRST_HALF if to_right else SECOND_HALF

    def prepare(step, chunk, to_right):
        if to_right:
            target = lax.rem(me + half - step, blocks)
        else:
            target = lax.rem(me - half + step + blocks, blocks)
        way = 0 if to_right else 1
        ready_ref[step % 2, way, pl.ds(*CHUNKS[chunk]), :] = contribution(target, chunk)

    def advance(step, chunk, to_right):
        rows = pl.ds(*CHUNKS[chunk])
        going, coming = (out_r, in_r) if to_right else (out_l, in_l)
        total = ready_ref[step % 2, 0 if to_right else 1, rows, :]
        if step > 0 and chunk in reduced(step - 1, to_right):
            reduce_copy(step - 1, chunk, to_right).wait_recv()
            total = total + coming[step - 1, rows, :].astype(F32)
        going[step, rows, :] = total.astype(BF16)
        item = reduce_copy(step, chunk, to_right)
        item.start()
        started.append(item)

    own = []
    for step in range(half):
        for index in range(len(ALL_CHUNKS)):
            for to_right in (True, False):
                chunk = ALL_CHUNKS[index if to_right else -1 - index]
                if chunk in reduced(step, to_right):
                    if step == 0:
                        prepare(step, chunk, to_right)
                    advance(step, chunk, to_right)
                if step > 0 and step + 1 < half:
                    prepare(step + 1, chunk, to_right)
            if step == half - 1:
                own.append(contribution(me, ALL_CHUNKS[index]))
        if step == 0:
            for index in range(len(ALL_CHUNKS)):
                for to_right in (True, False):
                    prepare(1, ALL_CHUNKS[index if to_right else -1 - index], to_right)
    for chunk in ALL_CHUNKS:
        for to_right in (True, False):
            reduce_copy(half - 1, chunk, to_right).wait_recv()
    own = jnp.concatenate(own, axis=0)
    for chan in range(2):
        rows = pl.ds(chan * CHAN_ROWS, CHAN_ROWS)
        total = in_r[half - 1, rows, :].astype(F32) + in_l[half - 1, rows, :].astype(F32)
        total = total + own[chan * CHAN_ROWS : (chan + 1) * CHAN_ROWS]
        for z in range(LAYERS):
            out_ref[chan, pl.ds(z, TH, stride=LAYERS), :] = total[z * TH : (z + 1) * TH]
    for item in started:
        item.wait_send()


VMEM = pl.BlockSpec(memory_space=pltpu.VMEM)
HBM = pl.BlockSpec(memory_space=pltpu.HBM)


def on_device(delta_obj, beta_obj, layer_shifts, field, amplitudes, positions, counts):
    blocks = lax.axis_size("ang")
    tiles = lax.axis_size("rows")
    half = blocks // 2
    table = pltpu.VMEM((2 * PIX, 2 * PIX), BF16)
    stage = pltpu.VMEM((half, BLOCK_ROWS, COLS), BF16)
    ring_sems = pltpu.SemaphoreType.DMA((half, len(CHUNKS)))
    pos = jnp.swapaxes(positions, 1, 2)
    grad = pl.pallas_call(
        functools.partial(kernel, blocks, tiles),
        out_shape=jax.ShapeDtypeStruct((2, CHAN_ROWS, COLS), F32),
        in_specs=[HBM] * 11,
        out_specs=VMEM,
        scratch_shapes=[
            pltpu.VMEM((2, CHAN_ROWS, COLS), F32),
            pltpu.VMEM((2, PIX, PIX), F32),
            pltpu.VMEM((STRIPS, PIX, PIX), F32),
            table,
            table,
            table,
            table,
            pltpu.SMEM((LAYERS, blocks), jnp.int32),
            pltpu.SMEM((1, 2, SLOTS), jnp.int32),
            pltpu.SMEM((1, 1), jnp.int32),
            pltpu.VMEM((2, SLOTS), jnp.int32),
            pltpu.SMEM((2, SLOTS), jnp.int32),
            pltpu.VMEM((blocks, BLOCK_ROWS, COLS), BF16),
            pltpu.VMEM((SLOTS - 1, 2, TH, PIX), F32),
            pltpu.VMEM((2, 2 * TH, PIX), F32),
            pltpu.VMEM((2, 2 * TH, PIX), F32),
            pltpu.VMEM((STRIPS, 2, PIX, PIX), F32),
            pltpu.VMEM((STRIPS, 2, 2 * TH, PIX), F32),
            pltpu.VMEM((STRIPS, BLOCK_ROWS, COLS), F32),
            stage,
            stage,
            stage,
            stage,
            pltpu.SemaphoreType.DMA((12,)),
            pltpu.SemaphoreType.DMA((6,)),
            pltpu.SemaphoreType.DMA((6,)),
        ]
        + [ring_sems] * 8
        + [pltpu.VMEM((2, 2, BLOCK_ROWS, COLS), F32)],
        compiler_params=pltpu.CompilerParams(
            vmem_limit_bytes=67043328, collective_id=0, has_side_effects=True
        ),
    )(
        delta_obj.reshape(CHAN_ROWS, COLS),
        beta_obj.reshape(CHAN_ROWS, COLS),
        field,
        amplitudes,
        *dft_constants(),
        layer_shifts.T,
        pos,
        counts,
    )
    shape = (TH, LAYERS, COLS)
    return (grad[0].reshape(shape), grad[1].reshape(shape))


def solution(mesh):
    placed = (
        P("rows", None, "ang"),
        P("rows", None, "ang"),
        P(),
        P(),
        P("ang", "rows", None, None),
        P("ang", "rows", None),
        P("ang", "rows"),
    )
    return jax.shard_map(
        on_device,
        mesh=mesh,
        in_specs=placed,
        out_specs=(P("rows", None, "ang"), P("rows", None, "ang")),
        check_vma=False,
    )
```

```python
import functools
import math

import jax
import jax.numpy as jnp
import numpy as np
from jax import lax
from jax.experimental import pallas as pl
from jax.experimental.pallas import tpu as pltpu
from jax.sharding import PartitionSpec as P

PIX = 128
TH = 136
COLS = 128
LAYERS = 2
SHIFT = 8
SLOTS = 4
AMP_FLOOR = 0.1
BLOCK_ROWS = 2 * LAYERS * TH
CHAN_ROWS = LAYERS * TH
F32 = jnp.float32
BF16 = jnp.bfloat16


def dft_constants():
    counter = np.arange(PIX)
    angle = (counter[:, None] * counter[None, :] % PIX) * (2.0 * math.pi / PIX)
    scale = 1.0 / math.sqrt(PIX)
    re = np.cos(angle) * scale
    im = -np.sin(angle) * scale
    m1 = np.block([[re, -im], [im, re]])
    m2 = np.block([[re, im], [-im, re]])

    def split(m):
        hi = m.astype(BF16)
        lo = (m - hi.astype(np.float64)).astype(BF16)
        return np.asarray(hi), np.asarray(lo)

    return split(m1) + split(m2)


def split_f32(x):
    hi = x.astype(BF16)
    lo = (x - hi.astype(F32)).astype(BF16)
    return hi, lo


def dot(a, b):
    return jnp.dot(a, b, preferred_element_type=F32)


def left_product(hi, lo, data):
    d_hi, d_lo = split_f32(data)
    return dot(hi, d_hi) + (dot(hi, d_lo) + dot(lo, d_hi))


def right_product(data, hi, lo):
    d_hi, d_lo = split_f32(data)
    return dot(d_hi, hi) + (dot(d_lo, hi) + dot(d_hi, lo))


def sin_cos(x):
    k = jnp.floor(x * (2.0 / math.pi) + 0.5)
    y = x - k * 1.5703125
    y = y - k * 4.837512969970703125e-4
    y = y - k * 7.54978995489188216e-8
    q = k.astype(jnp.int32)
    y2 = y * y
    s = y + y * y2 * (-1.6666654611e-1 + y2 * (8.3321608736e-3 + y2 * -1.9515295891e-4))
    c = (1.0 - 0.5 * y2) + y2 * y2 * (
        4.166664568298827e-2 + y2 * (-1.388731625493765e-3 + y2 * 2.443315711809948e-5)
    )
    odd = (q & 1) == 1
    sn = jnp.where(odd, c, s)
    cs = jnp.where(odd, s, c)
    sn = jnp.where((q & 2) == 2, -sn, sn)
    cs = jnp.where(((q + 1) & 2) == 2, -cs, cs)
    return sn, cs


def place(col, shift, blocks):
    start = col + shift
    start = jnp.where(start < 0, start + blocks * COLS, start)
    first = jnp.right_shift(start, 7)
    offset = start & (COLS - 1)
    second = jnp.where(first == blocks - 1, 0, first + 1)
    return first, second, offset


PARTS = (144, 128)


def chunk_table():
    table, start = [], 0
    for size in PARTS * 2:
        table.append((start, size))
        start += size
    return tuple(table)


CHUNKS = chunk_table()
ALL_CHUNKS = tuple(range(len(CHUNKS)))
FIRST_HALF = ALL_CHUNKS[: len(PARTS)]
SECOND_HALF = ALL_CHUNKS[len(PARTS) :]
STRIPS = SLOTS + 1
PREV = SLOTS


def kernel(
    blocks,
    tiles,
    delta_hbm,
    beta_hbm,
    field_hbm,
    amp_hbm,
    m1h_hbm,
    m1l_hbm,
    m2h_hbm,
    m2l_hbm,
    shifts_hbm,
    pos_hbm,
    count_hbm,
    out_ref,
    object_ref,
    field_ref,
    amp_ref,
    m1h_ref,
    m1l_ref,
    m2h_ref,
    m2l_ref,
    shifts_ref,
    pos_ref,
    count_ref,
    prev_pos_vmem,
    prev_pos,
    g_ref,
    strip_ref,
    strip_own,
    strip_prev,
    trans_ref,
    back_ref,
    rolled_ref,
    out_r,
    out_l,
    in_r,
    in_l,
    load_sem,
    edge_send,
    edge_recv,
    send_r,
    recv_r,
    send_l,
    recv_l,
    send_r2,
    recv_r2,
    send_l2,
    recv_l2,
    ready_ref,
    edge_out,
    edge_in,
):
    me = lax.axis_index("ang")
    right = lax.rem(me + 1, blocks)
    left = lax.rem(me + blocks - 1, blocks)
    tile = lax.axis_index("rows")
    below = lax.rem(tile + 1, tiles)
    above = lax.rem(tile + tiles - 1, tiles)
    half = blocks // 2

    loads = [
        pltpu.make_async_copy(src, dst, load_sem.at[i])
        for i, (src, dst) in enumerate(
            (
                (delta_hbm, object_ref.at[0]),
                (beta_hbm, object_ref.at[1]),
                (amp_hbm.at[0], amp_ref.at[pl.ds(0, SLOTS)]),
                (field_hbm, field_ref),
                (m1h_hbm, m1h_ref),
                (m1l_hbm, m1l_ref),
                (m2h_hbm, m2h_ref),
                (m2l_hbm, m2l_ref),
                (shifts_hbm, shifts_ref),
                (pos_hbm, pos_ref),
                (count_hbm, count_ref),
            )
        )
    ]
    for item in loads:
        item.start()
    barrier = pltpu.get_barrier_semaphore()
    for target in ({"ang": left}, {"ang": right}, {"rows": above}, {"rows": below}):
        pl.semaphore_signal(barrier, inc=1, device_id=target)
    for chan in range(2):
        loads[chan].wait()
        layers = [object_ref[chan, pl.ds(z, TH, stride=LAYERS), :] for z in range(LAYERS)]
        rows = pl.ds(chan * CHAN_ROWS, CHAN_ROWS)
        g_ref[me, rows, :] = jnp.concatenate(layers, axis=0).astype(BF16)
    pl.semaphore_wait(barrier, 4)

    def remote(src, dst, send_sem, recv_sem, target):
        return pltpu.make_async_remote_copy(
            src_ref=src, dst_ref=dst, send_sem=send_sem, recv_sem=recv_sem, device_id=target
        )

    def edge(index, src, dst, target):
        return remote(src, dst, edge_send.at[index], edge_recv.at[index], target)

    def gather_copy(step, chunk, to_right, coming=False):
        hops = step + 1 if coming else step
        if to_right:
            origin = lax.rem(me - hops + blocks, blocks)
        else:
            origin = lax.rem(me + hops, blocks)
        part = g_ref.at[origin, pl.ds(*CHUNKS[chunk]), :]
        if to_right:
            return remote(
                part, part, send_r.at[step, chunk], recv_r.at[step, chunk], {"ang": right}
            )
        return remote(part, part, send_l.at[step, chunk], recv_l.at[step, chunk], {"ang": left})

    def gathered(step, to_right):
        if step < half - 1:
            return ALL_CHUNKS
        return FIRST_HALF if to_right else SECOND_HALF

    pos_edge = edge(0, pos_hbm.at[0], prev_pos_vmem, {"rows": below})
    amp_edge = edge(1, amp_hbm.at[0, 0], amp_ref.at[PREV], {"rows": below})
    started = [pos_edge, amp_edge]
    for step in range(half):
        for index in range(len(ALL_CHUNKS)):
            for to_right in (True, False):
                chunk = ALL_CHUNKS[index if to_right else -1 - index]
                if step > 0:
                    gather_copy(step - 1, chunk, to_right, coming=True).wait_recv()
                if chunk in gathered(step, to_right):
                    item = gather_copy(step, chunk, to_right)
                    item.start()
                    started.append(item)
        if step == 0:
            pos_edge.start()
            amp_edge.start()
        if step == 3:
            pos_edge.wait_recv()
            prev_load = pltpu.make_async_copy(prev_pos_vmem, prev_pos, load_sem.at[11])
            prev_load.start()
    for item in loads[2:]:
        item.wait()
    prev_load.wait()
    amp_edge.wait_recv()
    for to_right in (True, False):
        for chunk in gathered(half - 1, to_right):
            gather_copy(half - 1, chunk, to_right, coming=True).wait_recv()

    lane = lax.broadcasted_iota(jnp.int32, (TH, COLS), 1)
    cols, firsts, seconds, offsets, row_starts = [], [], [], [], []
    for slot in range(STRIPS):
        row = prev_pos[0, 0] if slot == PREV else pos_ref[0, 0, slot]
        col = prev_pos[1, 0] if slot == PREV else pos_ref[0, 1, slot]
        row_starts.append(jnp.clip(row, 0, TH if slot in (0, PREV) else TH - PIX))
        cols.append(jnp.clip(col, 0, blocks * COLS - PIX))
        spots = [place(cols[slot], shifts_ref[z, me], blocks) for z in range(LAYERS)]
        firsts.append([spot[0] for spot in spots])
        seconds.append([spot[1] for spot in spots])
        offsets.append([spot[2] for spot in spots])

    def strip(slot, chan):
        total = None
        for z in range(LAYERS):
            rows = pl.ds(chan * CHAN_ROWS, CHAN_ROWS)
            offset = offsets[slot][z]
            part0 = g_ref[firsts[slot][z], rows, :].astype(F32)[z * TH : (z + 1) * TH]
            part1 = g_ref[seconds[slot][z], rows, :].astype(F32)[z * TH : (z + 1) * TH]
            both = jnp.where(lane >= offset, part0, part1)
            value = pltpu.roll(both, (COLS - offset) & (COLS - 1), 1)
            total = value if total is None else total + value
        return total

    lower = pl.ds(TH, PIX)
    upper = pl.ds(SHIFT, PIX)
    strip_edges = []
    for chan in range(2):
        strip_prev[chan, TH:] = strip(PREV, chan)
        strip_prev[chan, :SHIFT] = jnp.zeros((SHIFT, COLS), F32)
        strip_own[chan, :TH] = strip(0, chan)
        edge_out[chan, 0] = strip_prev[chan, lower, :].astype(BF16)
        edge_out[chan, 1] = strip_own[chan, upper, :].astype(BF16)
        strip_edges += [
            edge(2 + chan, edge_out.at[chan, 0], edge_in.at[chan, 0], {"rows": above}),
            edge(4 + chan, edge_out.at[chan, 1], edge_in.at[chan, 1], {"rows": below}),
        ]
        for item in strip_edges[-2:]:
            item.start()
    started += strip_edges
    for slot in range(1, SLOTS):
        for chan in range(2):
            strip_ref[slot - 1, chan] = strip(slot, chan)

    probe_re = field_ref[0]
    probe_im = field_ref[1]
    depth = lax.broadcasted_iota(jnp.int32, (PIX, PIX), 0)

    def patch(slot, chan):
        rows = pl.ds(row_starts[slot], PIX)
        if slot == PREV:
            return strip_prev[chan, rows, :]
        if slot > 0:
            return strip_ref[slot - 1, chan, rows, :]
        value = strip_own[chan, rows, :]
        outside = (depth + row_starts[slot] >= TH) & (tile == tiles - 1)
        return jnp.where(outside, 0.0, value)

    def scans(slots):
        number = len(slots)
        exit_re, exit_im = [], []
        for slot in slots:
            damping = jnp.exp(-patch(slot, 1))
            sn, cs = sin_cos(patch(slot, 0))
            tre = damping * cs
            tim = damping * sn
            trans_ref[slot, 0] = tre
            trans_ref[slot, 1] = tim
            exit_re.append(probe_re * tre - probe_im * tim)
            exit_im.append(probe_re * tim + probe_im * tre)
        data = jnp.concatenate(
            [jnp.concatenate(exit_re, axis=1), jnp.concatenate(exit_im, axis=1)], axis=0
        )
        wide = left_product(m1h_ref[...], m1l_ref[...], data)
        wide = jnp.concatenate(
            [
                jnp.concatenate(
                    [wide[:PIX, j * PIX : (j + 1) * PIX], wide[PIX:, j * PIX : (j + 1) * PIX]],
                    axis=1,
                )
                for j in range(number)
            ],
            axis=0,
        )
        far = right_product(wide, m2h_ref[...], m2l_ref[...])
        residual = []
        for j, slot in enumerate(slots):
            rows = far[j * PIX : (j + 1) * PIX]
            re, im = rows[:, :PIX], rows[:, PIX:]
            live = tile > 0 if slot == PREV else slot < count_ref[0, 0]
            inverse = lax.rsqrt(jnp.maximum(re * re + im * im, AMP_FLOOR * AMP_FLOOR))
            factor = jnp.where(live, 1.0 - amp_ref[slot] * inverse, 0.0)
            residual.append(jnp.concatenate([re * factor, im * factor], axis=1))
        back = right_product(jnp.concatenate(residual, axis=0), m1h_ref[...], m1l_ref[...])
        tall = jnp.concatenate(
            [
                jnp.concatenate([back[j * PIX : (j + 1) * PIX, :PIX] for j in range(number)], axis=1),
                jnp.concatenate([back[j * PIX : (j + 1) * PIX, PIX:] for j in range(number)], axis=1),
            ],
            axis=0,
        )
        grad = left_product(m2h_ref[...], m2l_ref[...], tall)
        for j, slot in enumerate(slots):
            bre = grad[:PIX, j * PIX : (j + 1) * PIX]
            bim = grad[PIX:, j * PIX : (j + 1) * PIX]
            gre = probe_re * bre + probe_im * bim
            gim = probe_re * bim - probe_im * bre
            tre = trans_ref[slot, 0]
            tim = trans_ref[slot, 1]
            at = TH if slot == 0 else 0 if slot == PREV else SHIFT
            bottom = SHIFT if slot != PREV else TH + SHIFT
            start = (SHIFT if slot in range(1, SLOTS) else TH) - row_starts[slot]
            for chan, value in enumerate((tre * gim - tim * gre, -(tre * gre + tim * gim))):
                if at:
                    back_ref[slot, chan, :at] = jnp.zeros((at, PIX), F32)
                back_ref[slot, chan, at : at + PIX] = value
                back_ref[slot, chan, at + PIX : at + PIX + bottom] = jnp.zeros((bottom, PIX), F32)
                placed = back_ref[slot, chan, pl.ds(start, TH), :]
                for z in range(LAYERS):
                    first_row = chan * CHAN_ROWS + z * TH
                    rolled_ref[slot, first_row : first_row + TH] = pltpu.roll(
                        placed, offsets[slot][z], 1
                    )

    for item in strip_edges:
        item.wait_recv()
    for chan in range(2):
        strip_own[chan, lower, :] = edge_in[chan, 0].astype(F32)
        strip_prev[chan, upper, :] = edge_in[chan, 1].astype(F32)
    scans((1, 2, 3, 0, PREV))

    line = lax.broadcasted_iota(jnp.int32, (8, COLS), 1)

    def contribution(target, chunk):
        begin, size = CHUNKS[chunk]
        pieces = []
        for z_start in range(0, BLOCK_ROWS, TH):
            low, high = max(begin, z_start), min(begin + size, z_start + TH)
            if low >= high:
                continue
            z = (z_start // TH) % LAYERS
            total = None
            for slot in range(STRIPS):
                offset = offsets[slot][z]
                in_first = target == firsts[slot][z]
                in_second = target == seconds[slot][z]
                least = jnp.where(in_first, offset, jnp.where(in_second, 0, COLS))
                most = jnp.where(in_first, COLS, jnp.where(in_second, offset, 0))
                inside = (lane[: high - low] >= least) & (lane[: high - low] < most)
                value = jnp.where(inside, rolled_ref[slot, low:high], 0.0)
                total = value if total is None else total + value
            pieces.append(total)
        return jnp.concatenate(pieces, axis=0) if len(pieces) > 1 else pieces[0]

    def reduce_copy(step, chunk, to_right):
        rows = pl.ds(*CHUNKS[chunk])
        if to_right:
            return remote(
                out_r.at[step, rows, :],
                in_r.at[step, rows, :],
                send_r2.at[step, chunk],
                recv_r2.at[step, chunk],
                {"ang": right},
            )
        return remote(
            out_l.at[step, rows, :],
            in_l.at[step, rows, :],
            send_l2.at[step, chunk],
            recv_l2.at[step, chunk],
            {"ang": left},
        )

    def reduced(step, to_right):
        if step > 0:
            return ALL_CHUNKS
        return FIRST_HALF if to_right else SECOND_HALF

    def prepare(step, chunk, to_right):
        if to_right:
            target = lax.rem(me + half - step, blocks)
        else:
            target = lax.rem(me - half + step + blocks, blocks)
        way = 0 if to_right else 1
        ready_ref[step % 2, way, pl.ds(*CHUNKS[chunk]), :] = contribution(target, chunk)

    def advance(step, chunk, to_right):
        rows = pl.ds(*CHUNKS[chunk])
        going, coming = (out_r, in_r) if to_right else (out_l, in_l)
        total = ready_ref[step % 2, 0 if to_right else 1, rows, :]
        if step > 0 and chunk in reduced(step - 1, to_right):
            reduce_copy(step - 1, chunk, to_right).wait_recv()
            total = total + coming[step - 1, rows, :].astype(F32)
        going[step, rows, :] = total.astype(BF16)
        item = reduce_copy(step, chunk, to_right)
        item.start()
        started.append(item)

    own = []
    for step in range(half):
        for index in range(len(ALL_CHUNKS)):
            for to_right in (True, False):
                chunk = ALL_CHUNKS[index if to_right else -1 - index]
                if chunk in reduced(step, to_right):
                    if step == 0:
                        prepare(step, chunk, to_right)
                    advance(step, chunk, to_right)
                if step > 0 and step + 1 < half:
                    prepare(step + 1, chunk, to_right)
            if step == half - 1:
                own.append(contribution(me, ALL_CHUNKS[index]))
        if step == 0:
            for index in range(len(ALL_CHUNKS)):
                for to_right in (True, False):
                    prepare(1, ALL_CHUNKS[index if to_right else -1 - index], to_right)
    for chunk in ALL_CHUNKS:
        for to_right in (True, False):
            reduce_copy(half - 1, chunk, to_right).wait_recv()
    own = jnp.concatenate(own, axis=0)
    for chan in range(2):
        rows = pl.ds(chan * CHAN_ROWS, CHAN_ROWS)
        total = in_r[half - 1, rows, :].astype(F32) + in_l[half - 1, rows, :].astype(F32)
        total = total + own[chan * CHAN_ROWS : (chan + 1) * CHAN_ROWS]
        for z in range(LAYERS):
            out_ref[chan, pl.ds(z, TH, stride=LAYERS), :] = total[z * TH : (z + 1) * TH]
    for item in started:
        item.wait_send()


VMEM = pl.BlockSpec(memory_space=pltpu.VMEM)
HBM = pl.BlockSpec(memory_space=pltpu.HBM)


def on_device(delta_obj, beta_obj, layer_shifts, field, amplitudes, positions, counts):
    blocks = lax.axis_size("ang")
    tiles = lax.axis_size("rows")
    half = blocks // 2
    table = pltpu.VMEM((2 * PIX, 2 * PIX), BF16)
    stage = pltpu.VMEM((half, BLOCK_ROWS, COLS), BF16)
    ring_sems = pltpu.SemaphoreType.DMA((half, len(CHUNKS)))
    pos = jnp.swapaxes(positions, 1, 2)
    grad = pl.pallas_call(
        functools.partial(kernel, blocks, tiles),
        out_shape=jax.ShapeDtypeStruct((2, CHAN_ROWS, COLS), F32),
        in_specs=[HBM] * 11,
        out_specs=VMEM,
        scratch_shapes=[
            pltpu.VMEM((2, CHAN_ROWS, COLS), F32),
            pltpu.VMEM((2, PIX, PIX), F32),
            pltpu.VMEM((STRIPS, PIX, PIX), F32),
            table,
            table,
            table,
            table,
            pltpu.SMEM((LAYERS, blocks), jnp.int32),
            pltpu.SMEM((1, 2, SLOTS), jnp.int32),
            pltpu.SMEM((1, 1), jnp.int32),
            pltpu.VMEM((2, SLOTS), jnp.int32),
            pltpu.SMEM((2, SLOTS), jnp.int32),
            pltpu.VMEM((blocks, BLOCK_ROWS, COLS), BF16),
            pltpu.VMEM((SLOTS - 1, 2, TH, PIX), F32),
            pltpu.VMEM((2, 2 * TH, PIX), F32),
            pltpu.VMEM((2, 2 * TH, PIX), F32),
            pltpu.VMEM((STRIPS, 2, PIX, PIX), F32),
            pltpu.VMEM((STRIPS, 2, 2 * TH, PIX), F32),
            pltpu.VMEM((STRIPS, BLOCK_ROWS, COLS), F32),
            stage,
            stage,
            stage,
            stage,
            pltpu.SemaphoreType.DMA((12,)),
            pltpu.SemaphoreType.DMA((6,)),
            pltpu.SemaphoreType.DMA((6,)),
        ]
        + [ring_sems] * 8
        + [pltpu.VMEM((2, 2, BLOCK_ROWS, COLS), F32)]
        + [pltpu.VMEM((2, 2, PIX, PIX), BF16)] * 2,
        compiler_params=pltpu.CompilerParams(
            vmem_limit_bytes=50331648, collective_id=0, has_side_effects=True
        ),
    )(
        *(
            pltpu.with_memory_space_constraint(value, pltpu.HBM)
            for value in (
                delta_obj.reshape(CHAN_ROWS, COLS),
                beta_obj.reshape(CHAN_ROWS, COLS),
                field,
                amplitudes,
                *(jnp.asarray(m) for m in dft_constants()),
                layer_shifts.T,
                pos,
            )
        ),
        counts,
    )
    shape = (TH, LAYERS, COLS)
    return (grad[0].reshape(shape), grad[1].reshape(shape))


def solution(mesh):
    placed = (
        P("rows", None, "ang"),
        P("rows", None, "ang"),
        P(),
        P(),
        P("ang", "rows", None, None),
        P("ang", "rows", None),
        P("ang", "rows"),
    )
    return jax.shard_map(
        on_device,
        mesh=mesh,
        in_specs=placed,
        out_specs=(P("rows", None, "ang"), P("rows", None, "ang")),
        check_vma=False,
    )
```

```python
import functools
import math

import jax
import jax.numpy as jnp
import numpy as np
from jax import lax
from jax.experimental import pallas as pl
from jax.experimental.pallas import tpu as pltpu
from jax.sharding import PartitionSpec as P

PIX = 128
TH = 136
COLS = 128
LAYERS = 2
SHIFT = 8
SLOTS = 4
AMP_FLOOR = 0.1
BLOCK_ROWS = 2 * LAYERS * TH
CHAN_ROWS = LAYERS * TH
F32 = jnp.float32
BF16 = jnp.bfloat16


def dft_constants():
    counter = np.arange(PIX)
    angle = (counter[:, None] * counter[None, :] % PIX) * (2.0 * math.pi / PIX)
    scale = 1.0 / math.sqrt(PIX)
    re = np.cos(angle) * scale
    im = -np.sin(angle) * scale
    m1 = np.block([[re, -im], [im, re]])
    m2 = np.block([[re, im], [-im, re]])

    def split(m):
        hi = m.astype(BF16)
        lo = (m - hi.astype(np.float64)).astype(BF16)
        return np.asarray(hi), np.asarray(lo)

    return split(m1) + split(m2)


def split_f32(x):
    hi = x.astype(BF16)
    lo = (x - hi.astype(F32)).astype(BF16)
    return hi, lo


def dot(a, b):
    return jnp.dot(a, b, preferred_element_type=F32)


def left_product(hi, lo, data):
    d_hi, d_lo = split_f32(data)
    return dot(hi, d_hi) + (dot(hi, d_lo) + dot(lo, d_hi))


def right_product(data, hi, lo):
    d_hi, d_lo = split_f32(data)
    return dot(d_hi, hi) + (dot(d_lo, hi) + dot(d_hi, lo))


def sin_cos(x):
    k = jnp.floor(x * (2.0 / math.pi) + 0.5)
    y = x - k * 1.5703125
    y = y - k * 4.837512969970703125e-4
    y = y - k * 7.54978995489188216e-8
    q = k.astype(jnp.int32)
    y2 = y * y
    s = y + y * y2 * (-1.6666654611e-1 + y2 * (8.3321608736e-3 + y2 * -1.9515295891e-4))
    c = (1.0 - 0.5 * y2) + y2 * y2 * (
        4.166664568298827e-2 + y2 * (-1.388731625493765e-3 + y2 * 2.443315711809948e-5)
    )
    odd = (q & 1) == 1
    sn = jnp.where(odd, c, s)
    cs = jnp.where(odd, s, c)
    sn = jnp.where((q & 2) == 2, -sn, sn)
    cs = jnp.where(((q + 1) & 2) == 2, -cs, cs)
    return sn, cs


def place(col, shift, blocks):
    start = col + shift
    start = jnp.where(start < 0, start + blocks * COLS, start)
    first = jnp.right_shift(start, 7)
    offset = start & (COLS - 1)
    second = jnp.where(first == blocks - 1, 0, first + 1)
    return first, second, offset


PARTS = (144, 128)


def chunk_table():
    table, start = [], 0
    for size in PARTS * 2:
        table.append((start, size))
        start += size
    return tuple(table)


CHUNKS = chunk_table()
ALL_CHUNKS = tuple(range(len(CHUNKS)))
FIRST_HALF = ALL_CHUNKS[: len(PARTS)]
SECOND_HALF = ALL_CHUNKS[len(PARTS) :]
STRIPS = SLOTS + 1
PREV = SLOTS


def kernel(
    blocks,
    tiles,
    delta_hbm,
    beta_hbm,
    field_hbm,
    amp_hbm,
    m1h_hbm,
    m1l_hbm,
    m2h_hbm,
    m2l_hbm,
    shifts_hbm,
    pos_hbm,
    count_hbm,
    out_ref,
    object_ref,
    field_ref,
    amp_ref,
    m1h_ref,
    m1l_ref,
    m2h_ref,
    m2l_ref,
    shifts_ref,
    pos_ref,
    count_ref,
    prev_pos_vmem,
    prev_pos,
    g_ref,
    strip_ref,
    strip_own,
    strip_prev,
    trans_ref,
    back_ref,
    rolled_ref,
    out_r,
    out_l,
    in_r,
    in_l,
    load_sem,
    edge_send,
    edge_recv,
    send_r,
    recv_r,
    send_l,
    recv_l,
    send_r2,
    recv_r2,
    send_l2,
    recv_l2,
    ready_ref,
    edge_out,
    edge_in,
):
    me = lax.axis_index("ang")
    right = lax.rem(me + 1, blocks)
    left = lax.rem(me + blocks - 1, blocks)
    tile = lax.axis_index("rows")
    below = lax.rem(tile + 1, tiles)
    above = lax.rem(tile + tiles - 1, tiles)
    half = blocks // 2

    loads = [
        pltpu.make_async_copy(src, dst, load_sem.at[i])
        for i, (src, dst) in enumerate(
            (
                (delta_hbm, object_ref.at[0]),
                (beta_hbm, object_ref.at[1]),
                (amp_hbm.at[0], amp_ref.at[pl.ds(0, SLOTS)]),
                (field_hbm, field_ref),
                (m1h_hbm, m1h_ref),
                (m1l_hbm, m1l_ref),
                (m2h_hbm, m2h_ref),
                (m2l_hbm, m2l_ref),
                (shifts_hbm, shifts_ref),
                (pos_hbm, pos_ref),
                (count_hbm, count_ref),
            )
        )
    ]
    for item in loads:
        item.start()
    barrier = pltpu.get_barrier_semaphore()
    for target in ({"ang": left}, {"ang": right}, {"rows": above}, {"rows": below}):
        pl.semaphore_signal(barrier, inc=1, device_id=target)
    for chan in range(2):
        loads[chan].wait()
        layers = [object_ref[chan, pl.ds(z, TH, stride=LAYERS), :] for z in range(LAYERS)]
        rows = pl.ds(chan * CHAN_ROWS, CHAN_ROWS)
        g_ref[me, rows, :] = jnp.concatenate(layers, axis=0).astype(BF16)
    pl.semaphore_wait(barrier, 4)

    def remote(src, dst, send_sem, recv_sem, target):
        return pltpu.make_async_remote_copy(
            src_ref=src, dst_ref=dst, send_sem=send_sem, recv_sem=recv_sem, device_id=target
        )

    def edge(index, src, dst, target):
        return remote(src, dst, edge_send.at[index], edge_recv.at[index], target)

    def gather_copy(step, chunk, to_right, coming=False):
        hops = step + 1 if coming else step
        if to_right:
            origin = lax.rem(me - hops + blocks, blocks)
        else:
            origin = lax.rem(me + hops, blocks)
        part = g_ref.at[origin, pl.ds(*CHUNKS[chunk]), :]
        if to_right:
            return remote(
                part, part, send_r.at[step, chunk], recv_r.at[step, chunk], {"ang": right}
            )
        return remote(part, part, send_l.at[step, chunk], recv_l.at[step, chunk], {"ang": left})

    def gathered(step, to_right):
        if step < half - 1:
            return ALL_CHUNKS
        return FIRST_HALF if to_right else SECOND_HALF

    pos_edge = edge(0, pos_hbm.at[0], prev_pos_vmem, {"rows": below})
    amp_edge = edge(1, amp_hbm.at[0, 0], amp_ref.at[PREV], {"rows": below})
    started = [pos_edge, amp_edge]
    for step in range(half):
        for index in range(len(ALL_CHUNKS)):
            for to_right in (True, False):
                chunk = ALL_CHUNKS[index if to_right else -1 - index]
                if step > 0:
                    gather_copy(step - 1, chunk, to_right, coming=True).wait_recv()
                if chunk in gathered(step, to_right):
                    item = gather_copy(step, chunk, to_right)
                    item.start()
                    started.append(item)
        if step == 0:
            pos_edge.start()
            amp_edge.start()
        if step == 3:
            pos_edge.wait_recv()
            prev_load = pltpu.make_async_copy(prev_pos_vmem, prev_pos, load_sem.at[11])
            prev_load.start()
    for item in loads[2:]:
        item.wait()
    prev_load.wait()
    amp_edge.wait_recv()
    for to_right in (True, False):
        for chunk in gathered(half - 1, to_right):
            gather_copy(half - 1, chunk, to_right, coming=True).wait_recv()

    lane = lax.broadcasted_iota(jnp.int32, (TH, COLS), 1)
    cols, firsts, seconds, offsets, row_starts = [], [], [], [], []
    for slot in range(STRIPS):
        row = prev_pos[0, 0] if slot == PREV else pos_ref[0, 0, slot]
        col = prev_pos[1, 0] if slot == PREV else pos_ref[0, 1, slot]
        row_starts.append(jnp.clip(row, 0, TH if slot in (0, PREV) else TH - PIX))
        cols.append(jnp.clip(col, 0, blocks * COLS - PIX))
        spots = [place(cols[slot], shifts_ref[z, me], blocks) for z in range(LAYERS)]
        firsts.append([spot[0] for spot in spots])
        seconds.append([spot[1] for spot in spots])
        offsets.append([spot[2] for spot in spots])

    def strip(slot, chan):
        total = None
        for z in range(LAYERS):
            rows = pl.ds(chan * CHAN_ROWS, CHAN_ROWS)
            offset = offsets[slot][z]
            part0 = g_ref[firsts[slot][z], rows, :].astype(F32)[z * TH : (z + 1) * TH]
            part1 = g_ref[seconds[slot][z], rows, :].astype(F32)[z * TH : (z + 1) * TH]
            both = jnp.where(lane >= offset, part0, part1)
            value = pltpu.roll(both, (COLS - offset) & (COLS - 1), 1)
            total = value if total is None else total + value
        return total

    lower = pl.ds(TH, PIX)
    upper = pl.ds(SHIFT, PIX)
    strip_edges = []
    for chan in range(2):
        strip_prev[chan, TH:] = strip(PREV, chan)
        strip_prev[chan, :SHIFT] = jnp.zeros((SHIFT, COLS), F32)
        strip_own[chan, :TH] = strip(0, chan)
        edge_out[chan, 0] = strip_prev[chan, lower, :].astype(BF16)
        edge_out[chan, 1] = strip_own[chan, upper, :].astype(BF16)
        strip_edges += [
            edge(2 + chan, edge_out.at[chan, 0], edge_in.at[chan, 0], {"rows": above}),
            edge(4 + chan, edge_out.at[chan, 1], edge_in.at[chan, 1], {"rows": below}),
        ]
        for item in strip_edges[-2:]:
            item.start()
    started += strip_edges
    for slot in range(1, SLOTS):
        for chan in range(2):
            strip_ref[slot - 1, chan] = strip(slot, chan)

    probe_re = field_ref[0]
    probe_im = field_ref[1]
    depth = lax.broadcasted_iota(jnp.int32, (PIX, PIX), 0)

    def patch(slot, chan):
        rows = pl.ds(row_starts[slot], PIX)
        if slot == PREV:
            return strip_prev[chan, rows, :]
        if slot > 0:
            return strip_ref[slot - 1, chan, rows, :]
        value = strip_own[chan, rows, :]
        outside = (depth + row_starts[slot] >= TH) & (tile == tiles - 1)
        return jnp.where(outside, 0.0, value)

    def scans(slots):
        number = len(slots)
        exit_re, exit_im = [], []
        for slot in slots:
            damping = jnp.exp(-patch(slot, 1))
            sn, cs = sin_cos(patch(slot, 0))
            tre = damping * cs
            tim = damping * sn
            trans_ref[slot, 0] = tre
            trans_ref[slot, 1] = tim
            exit_re.append(probe_re * tre - probe_im * tim)
            exit_im.append(probe_re * tim + probe_im * tre)
        data = jnp.concatenate(
            [jnp.concatenate(exit_re, axis=1), jnp.concatenate(exit_im, axis=1)], axis=0
        )
        wide = left_product(m1h_ref[...], m1l_ref[...], data)
        wide = jnp.concatenate(
            [
                jnp.concatenate(
                    [wide[:PIX, j * PIX : (j + 1) * PIX], wide[PIX:, j * PIX : (j + 1) * PIX]],
                    axis=1,
                )
                for j in range(number)
            ],
            axis=0,
        )
        far = right_product(wide, m2h_ref[...], m2l_ref[...])
        residual = []
        for j, slot in enumerate(slots):
            rows = far[j * PIX : (j + 1) * PIX]
            re, im = rows[:, :PIX], rows[:, PIX:]
            live = tile > 0 if slot == PREV else slot < count_ref[0, 0]
            inverse = lax.rsqrt(jnp.maximum(re * re + im * im, AMP_FLOOR * AMP_FLOOR))
            factor = jnp.where(live, 1.0 - amp_ref[slot] * inverse, 0.0)
            residual.append(jnp.concatenate([re * factor, im * factor], axis=1))
        back = right_product(jnp.concatenate(residual, axis=0), m1h_ref[...], m1l_ref[...])
        tall = jnp.concatenate(
            [
                jnp.concatenate([back[j * PIX : (j + 1) * PIX, :PIX] for j in range(number)], axis=1),
                jnp.concatenate([back[j * PIX : (j + 1) * PIX, PIX:] for j in range(number)], axis=1),
            ],
            axis=0,
        )
        grad = left_product(m2h_ref[...], m2l_ref[...], tall)
        for j, slot in enumerate(slots):
            bre = grad[:PIX, j * PIX : (j + 1) * PIX]
            bim = grad[PIX:, j * PIX : (j + 1) * PIX]
            gre = probe_re * bre + probe_im * bim
            gim = probe_re * bim - probe_im * bre
            tre = trans_ref[slot, 0]
            tim = trans_ref[slot, 1]
            at = TH if slot == 0 else 0 if slot == PREV else SHIFT
            bottom = SHIFT if slot != PREV else TH + SHIFT
            start = (SHIFT if slot in range(1, SLOTS) else TH) - row_starts[slot]
            for chan, value in enumerate((tre * gim - tim * gre, -(tre * gre + tim * gim))):
                if at:
                    back_ref[slot, chan, :at] = jnp.zeros((at, PIX), F32)
                back_ref[slot, chan, at : at + PIX] = value
                back_ref[slot, chan, at + PIX : at + PIX + bottom] = jnp.zeros((bottom, PIX), F32)
                placed = back_ref[slot, chan, pl.ds(start, TH), :]
                for z in range(LAYERS):
                    first_row = chan * CHAN_ROWS + z * TH
                    rolled_ref[slot, first_row : first_row + TH] = pltpu.roll(
                        placed, offsets[slot][z], 1
                    )

    def receive_strips():
        for item in strip_edges:
            item.wait_recv()
        for chan in range(2):
            strip_own[chan, lower, :] = edge_in[chan, 0].astype(F32)
            strip_prev[chan, upper, :] = edge_in[chan, 1].astype(F32)

    far_strip = lax.rem(tile, 2) == 1

    @pl.when(far_strip)
    def _():
        scans((1, 2, 3))
        receive_strips()
        scans((0, PREV))

    @pl.when(jnp.logical_not(far_strip))
    def _():
        receive_strips()
        scans((1, 2, 3, 0, PREV))

    line = lax.broadcasted_iota(jnp.int32, (8, COLS), 1)

    def contribution(target, chunk):
        begin, size = CHUNKS[chunk]
        pieces = []
        for z_start in range(0, BLOCK_ROWS, TH):
            low, high = max(begin, z_start), min(begin + size, z_start + TH)
            if low >= high:
                continue
            z = (z_start // TH) % LAYERS
            total = None
            for slot in range(STRIPS):
                offset = offsets[slot][z]
                in_first = target == firsts[slot][z]
                in_second = target == seconds[slot][z]
                least = jnp.where(in_first, offset, jnp.where(in_second, 0, COLS))
                most = jnp.where(in_first, COLS, jnp.where(in_second, offset, 0))
                inside = (lane[: high - low] >= least) & (lane[: high - low] < most)
                value = jnp.where(inside, rolled_ref[slot, low:high], 0.0)
                total = value if total is None else total + value
            pieces.append(total)
        return jnp.concatenate(pieces, axis=0) if len(pieces) > 1 else pieces[0]

    def reduce_copy(step, chunk, to_right):
        rows = pl.ds(*CHUNKS[chunk])
        if to_right:
            return remote(
                out_r.at[step, rows, :],
                in_r.at[step, rows, :],
                send_r2.at[step, chunk],
                recv_r2.at[step, chunk],
                {"ang": right},
            )
        return remote(
            out_l.at[step, rows, :],
            in_l.at[step, rows, :],
            send_l2.at[step, chunk],
            recv_l2.at[step, chunk],
            {"ang": left},
        )

    def reduced(step, to_right):
        if step > 0:
            return ALL_CHUNKS
        return FIRST_HALF if to_right else SECOND_HALF

    def prepare(step, chunk, to_right):
        if to_right:
            target = lax.rem(me + half - step, blocks)
        else:
            target = lax.rem(me - half + step + blocks, blocks)
        way = 0 if to_right else 1
        ready_ref[step % 2, way, pl.ds(*CHUNKS[chunk]), :] = contribution(target, chunk)

    def advance(step, chunk, to_right):
        rows = pl.ds(*CHUNKS[chunk])
        going, coming = (out_r, in_r) if to_right else (out_l, in_l)
        total = ready_ref[step % 2, 0 if to_right else 1, rows, :]
        if step > 0 and chunk in reduced(step - 1, to_right):
            reduce_copy(step - 1, chunk, to_right).wait_recv()
            total = total + coming[step - 1, rows, :].astype(F32)
        going[step, rows, :] = total.astype(BF16)
        item = reduce_copy(step, chunk, to_right)
        item.start()
        started.append(item)

    own = []
    for step in range(half):
        for index in range(len(ALL_CHUNKS)):
            for to_right in (True, False):
                chunk = ALL_CHUNKS[index if to_right else -1 - index]
                if chunk in reduced(step, to_right):
                    if step == 0:
                        prepare(step, chunk, to_right)
                    advance(step, chunk, to_right)
                if step > 0 and step + 1 < half:
                    prepare(step + 1, chunk, to_right)
            if step == half - 1:
                own.append(contribution(me, ALL_CHUNKS[index]))
        if step == 0:
            for index in range(len(ALL_CHUNKS)):
                for to_right in (True, False):
                    prepare(1, ALL_CHUNKS[index if to_right else -1 - index], to_right)
    for chunk in ALL_CHUNKS:
        for to_right in (True, False):
            reduce_copy(half - 1, chunk, to_right).wait_recv()
    own = jnp.concatenate(own, axis=0)
    for chan in range(2):
        rows = pl.ds(chan * CHAN_ROWS, CHAN_ROWS)
        total = in_r[half - 1, rows, :].astype(F32) + in_l[half - 1, rows, :].astype(F32)
        total = total + own[chan * CHAN_ROWS : (chan + 1) * CHAN_ROWS]
        for z in range(LAYERS):
            out_ref[chan, pl.ds(z, TH, stride=LAYERS), :] = total[z * TH : (z + 1) * TH]
    for item in started:
        item.wait_send()


VMEM = pl.BlockSpec(memory_space=pltpu.VMEM)
HBM = pl.BlockSpec(memory_space=pltpu.HBM)


def on_device(delta_obj, beta_obj, layer_shifts, field, amplitudes, positions, counts):
    blocks = lax.axis_size("ang")
    tiles = lax.axis_size("rows")
    half = blocks // 2
    table = pltpu.VMEM((2 * PIX, 2 * PIX), BF16)
    stage = pltpu.VMEM((half, BLOCK_ROWS, COLS), BF16)
    ring_sems = pltpu.SemaphoreType.DMA((half, len(CHUNKS)))
    pos = jnp.swapaxes(positions, 1, 2)
    grad = pl.pallas_call(
        functools.partial(kernel, blocks, tiles),
        out_shape=jax.ShapeDtypeStruct((2, CHAN_ROWS, COLS), F32),
        in_specs=[HBM] * 11,
        out_specs=VMEM,
        scratch_shapes=[
            pltpu.VMEM((2, CHAN_ROWS, COLS), F32),
            pltpu.VMEM((2, PIX, PIX), F32),
            pltpu.VMEM((STRIPS, PIX, PIX), F32),
            table,
            table,
            table,
            table,
            pltpu.SMEM((LAYERS, blocks), jnp.int32),
            pltpu.SMEM((1, 2, SLOTS), jnp.int32),
            pltpu.SMEM((1, 1), jnp.int32),
            pltpu.VMEM((2, SLOTS), jnp.int32),
            pltpu.SMEM((2, SLOTS), jnp.int32),
            pltpu.VMEM((blocks, BLOCK_ROWS, COLS), BF16),
            pltpu.VMEM((SLOTS - 1, 2, TH, PIX), F32),
            pltpu.VMEM((2, 2 * TH, PIX), F32),
            pltpu.VMEM((2, 2 * TH, PIX), F32),
            pltpu.VMEM((STRIPS, 2, PIX, PIX), F32),
            pltpu.VMEM((STRIPS, 2, 2 * TH, PIX), F32),
            pltpu.VMEM((STRIPS, BLOCK_ROWS, COLS), F32),
            stage,
            stage,
            stage,
            stage,
            pltpu.SemaphoreType.DMA((12,)),
            pltpu.SemaphoreType.DMA((6,)),
            pltpu.SemaphoreType.DMA((6,)),
        ]
        + [ring_sems] * 8
        + [pltpu.VMEM((2, 2, BLOCK_ROWS, COLS), F32)]
        + [pltpu.VMEM((2, 2, PIX, PIX), BF16)] * 2,
        compiler_params=pltpu.CompilerParams(
            vmem_limit_bytes=50331648, collective_id=0, has_side_effects=True
        ),
    )(
        *(
            pltpu.with_memory_space_constraint(value, pltpu.HBM)
            for value in (
                delta_obj.reshape(CHAN_ROWS, COLS),
                beta_obj.reshape(CHAN_ROWS, COLS),
                field,
                amplitudes,
                *(jnp.asarray(m) for m in dft_constants()),
                layer_shifts.T,
                pos,
            )
        ),
        counts,
    )
    shape = (TH, LAYERS, COLS)
    return (grad[0].reshape(shape), grad[1].reshape(shape))


def solution(mesh):
    placed = (
        P("rows", None, "ang"),
        P("rows", None, "ang"),
        P(),
        P(),
        P("ang", "rows", None, None),
        P("ang", "rows", None),
        P("ang", "rows"),
    )
    return jax.shard_map(
        on_device,
        mesh=mesh,
        in_specs=placed,
        out_specs=(P("rows", None, "ang"), P("rows", None, "ang")),
        check_vma=False,
    )
```

```python
import functools
import math

import jax
import jax.numpy as jnp
import numpy as np
from jax import lax
from jax.experimental import pallas as pl
from jax.experimental.pallas import tpu as pltpu
from jax.sharding import PartitionSpec as P

PIX = 128
TH = 136
COLS = 128
LAYERS = 2
SHIFT = 8
SLOTS = 4
AMP_FLOOR = 0.1
BLOCK_ROWS = 2 * LAYERS * TH
CHAN_ROWS = LAYERS * TH
F32 = jnp.float32
BF16 = jnp.bfloat16


def dft_constants():
    counter = np.arange(PIX)
    angle = (counter[:, None] * counter[None, :] % PIX) * (2.0 * math.pi / PIX)
    scale = 1.0 / math.sqrt(PIX)
    re = np.cos(angle) * scale
    im = -np.sin(angle) * scale
    m1 = np.block([[re, -im], [im, re]])
    m2 = np.block([[re, im], [-im, re]])

    def split(m):
        hi = m.astype(BF16)
        lo = (m - hi.astype(np.float64)).astype(BF16)
        return np.asarray(hi), np.asarray(lo)

    return split(m1) + split(m2)


def split_f32(x):
    hi = x.astype(BF16)
    lo = (x - hi.astype(F32)).astype(BF16)
    return hi, lo


def dot(a, b):
    return jnp.dot(a, b, preferred_element_type=F32)


def left_product(hi, lo, data):
    d_hi, d_lo = split_f32(data)
    return dot(hi, d_hi) + (dot(hi, d_lo) + dot(lo, d_hi))


def right_product(data, hi, lo):
    d_hi, d_lo = split_f32(data)
    return dot(d_hi, hi) + (dot(d_lo, hi) + dot(d_hi, lo))


def sin_cos(x):
    k = jnp.floor(x * (2.0 / math.pi) + 0.5)
    y = x - k * 1.5703125
    y = y - k * 4.837512969970703125e-4
    y = y - k * 7.54978995489188216e-8
    q = k.astype(jnp.int32)
    y2 = y * y
    s = y + y * y2 * (-1.6666654611e-1 + y2 * (8.3321608736e-3 + y2 * -1.9515295891e-4))
    c = (1.0 - 0.5 * y2) + y2 * y2 * (
        4.166664568298827e-2 + y2 * (-1.388731625493765e-3 + y2 * 2.443315711809948e-5)
    )
    odd = (q & 1) == 1
    sn = jnp.where(odd, c, s)
    cs = jnp.where(odd, s, c)
    sn = jnp.where((q & 2) == 2, -sn, sn)
    cs = jnp.where(((q + 1) & 2) == 2, -cs, cs)
    return sn, cs


def place(col, shift, blocks):
    start = col + shift
    start = jnp.where(start < 0, start + blocks * COLS, start)
    first = jnp.right_shift(start, 7)
    offset = start & (COLS - 1)
    second = jnp.where(first == blocks - 1, 0, first + 1)
    return first, second, offset


PARTS = (144, 128)


def chunk_table():
    table, start = [], 0
    for size in PARTS * 2:
        table.append((start, size))
        start += size
    return tuple(table)


CHUNKS = chunk_table()
ALL_CHUNKS = tuple(range(len(CHUNKS)))
FIRST_HALF = ALL_CHUNKS[: len(PARTS)]
SECOND_HALF = ALL_CHUNKS[len(PARTS) :]
STRIPS = SLOTS + 1
PREV = SLOTS


def kernel(
    blocks,
    tiles,
    delta_hbm,
    beta_hbm,
    field_hbm,
    amp_hbm,
    m1h_hbm,
    m1l_hbm,
    m2h_hbm,
    m2l_hbm,
    shifts_hbm,
    pos_hbm,
    count_hbm,
    out_ref,
    object_ref,
    field_ref,
    amp_ref,
    m1h_ref,
    m1l_ref,
    m2h_ref,
    m2l_ref,
    shifts_ref,
    pos_ref,
    count_ref,
    prev_pos_vmem,
    prev_pos,
    g_ref,
    strip_ref,
    strip_own,
    strip_prev,
    trans_ref,
    back_ref,
    rolled_ref,
    out_r,
    out_l,
    in_r,
    in_l,
    load_sem,
    edge_send,
    edge_recv,
    send_r,
    recv_r,
    send_l,
    recv_l,
    send_r2,
    recv_r2,
    send_l2,
    recv_l2,
    ready_ref,
    edge_out,
    edge_in,
):
    me = lax.axis_index("ang")
    right = lax.rem(me + 1, blocks)
    left = lax.rem(me + blocks - 1, blocks)
    tile = lax.axis_index("rows")
    below = lax.rem(tile + 1, tiles)
    above = lax.rem(tile + tiles - 1, tiles)
    half = blocks // 2

    loads = [
        pltpu.make_async_copy(src, dst, load_sem.at[i])
        for i, (src, dst) in enumerate(
            (
                (delta_hbm, object_ref.at[0]),
                (beta_hbm, object_ref.at[1]),
                (amp_hbm.at[0], amp_ref.at[pl.ds(0, SLOTS)]),
                (field_hbm, field_ref),
                (m1h_hbm, m1h_ref),
                (m1l_hbm, m1l_ref),
                (m2h_hbm, m2h_ref),
                (m2l_hbm, m2l_ref),
                (shifts_hbm, shifts_ref),
                (pos_hbm, pos_ref),
                (count_hbm, count_ref),
            )
        )
    ]
    for item in loads[:2]:
        item.start()
    barrier = pltpu.get_barrier_semaphore()
    for target in ({"ang": left}, {"ang": right}, {"rows": above}, {"rows": below}):
        pl.semaphore_signal(barrier, inc=1, device_id=target)
    for chan in range(2):
        loads[chan].wait()
        layers = [object_ref[chan, pl.ds(z, TH, stride=LAYERS), :] for z in range(LAYERS)]
        rows = pl.ds(chan * CHAN_ROWS, CHAN_ROWS)
        g_ref[me, rows, :] = jnp.concatenate(layers, axis=0).astype(BF16)
    pl.semaphore_wait(barrier, 4)

    def remote(src, dst, send_sem, recv_sem, target):
        return pltpu.make_async_remote_copy(
            src_ref=src, dst_ref=dst, send_sem=send_sem, recv_sem=recv_sem, device_id=target
        )

    def edge(index, src, dst, target):
        return remote(src, dst, edge_send.at[index], edge_recv.at[index], target)

    def gather_copy(step, chunk, to_right, coming=False):
        hops = step + 1 if coming else step
        if to_right:
            origin = lax.rem(me - hops + blocks, blocks)
        else:
            origin = lax.rem(me + hops, blocks)
        part = g_ref.at[origin, pl.ds(*CHUNKS[chunk]), :]
        if to_right:
            return remote(
                part, part, send_r.at[step, chunk], recv_r.at[step, chunk], {"ang": right}
            )
        return remote(part, part, send_l.at[step, chunk], recv_l.at[step, chunk], {"ang": left})

    def gathered(step, to_right):
        if step < half - 1:
            return ALL_CHUNKS
        return FIRST_HALF if to_right else SECOND_HALF

    pos_edge = edge(0, pos_hbm.at[0], prev_pos_vmem, {"rows": below})
    amp_edge = edge(1, amp_hbm.at[0, 0], amp_ref.at[PREV], {"rows": below})
    started = [pos_edge, amp_edge]
    for step in range(half):
        for index in range(len(ALL_CHUNKS)):
            for to_right in (True, False):
                chunk = ALL_CHUNKS[index if to_right else -1 - index]
                if step > 0:
                    gather_copy(step - 1, chunk, to_right, coming=True).wait_recv()
                if chunk in gathered(step, to_right):
                    item = gather_copy(step, chunk, to_right)
                    item.start()
                    started.append(item)
        if step == 0:
            for item in loads[2:]:
                item.start()
            pos_edge.start()
            amp_edge.start()
        if step == 3:
            pos_edge.wait_recv()
            prev_load = pltpu.make_async_copy(prev_pos_vmem, prev_pos, load_sem.at[11])
            prev_load.start()
    for item in loads[2:]:
        item.wait()
    prev_load.wait()
    amp_edge.wait_recv()
    for to_right in (True, False):
        for chunk in gathered(half - 1, to_right):
            gather_copy(half - 1, chunk, to_right, coming=True).wait_recv()

    lane = lax.broadcasted_iota(jnp.int32, (TH, COLS), 1)
    cols, firsts, seconds, offsets, row_starts = [], [], [], [], []
    for slot in range(STRIPS):
        row = prev_pos[0, 0] if slot == PREV else pos_ref[0, 0, slot]
        col = prev_pos[1, 0] if slot == PREV else pos_ref[0, 1, slot]
        row_starts.append(jnp.clip(row, 0, TH if slot in (0, PREV) else TH - PIX))
        cols.append(jnp.clip(col, 0, blocks * COLS - PIX))
        spots = [place(cols[slot], shifts_ref[z, me], blocks) for z in range(LAYERS)]
        firsts.append([spot[0] for spot in spots])
        seconds.append([spot[1] for spot in spots])
        offsets.append([spot[2] for spot in spots])

    def strip(slot, chan):
        total = None
        for z in range(LAYERS):
            rows = pl.ds(chan * CHAN_ROWS, CHAN_ROWS)
            offset = offsets[slot][z]
            part0 = g_ref[firsts[slot][z], rows, :].astype(F32)[z * TH : (z + 1) * TH]
            part1 = g_ref[seconds[slot][z], rows, :].astype(F32)[z * TH : (z + 1) * TH]
            both = jnp.where(lane >= offset, part0, part1)
            value = pltpu.roll(both, (COLS - offset) & (COLS - 1), 1)
            total = value if total is None else total + value
        return total

    lower = pl.ds(TH, PIX)
    upper = pl.ds(SHIFT, PIX)
    strip_edges = []
    for chan in range(2):
        strip_prev[chan, TH:] = strip(PREV, chan)
        strip_prev[chan, :SHIFT] = jnp.zeros((SHIFT, COLS), F32)
        strip_own[chan, :TH] = strip(0, chan)
        edge_out[chan, 0] = strip_prev[chan, lower, :].astype(BF16)
        edge_out[chan, 1] = strip_own[chan, upper, :].astype(BF16)
        strip_edges += [
            edge(2 + chan, edge_out.at[chan, 0], edge_in.at[chan, 0], {"rows": above}),
            edge(4 + chan, edge_out.at[chan, 1], edge_in.at[chan, 1], {"rows": below}),
        ]
        for item in strip_edges[-2:]:
            item.start()
    started += strip_edges
    for slot in range(1, SLOTS):
        for chan in range(2):
            strip_ref[slot - 1, chan] = strip(slot, chan)

    probe_re = field_ref[0]
    probe_im = field_ref[1]
    depth = lax.broadcasted_iota(jnp.int32, (PIX, PIX), 0)

    def patch(slot, chan):
        rows = pl.ds(row_starts[slot], PIX)
        if slot == PREV:
            return strip_prev[chan, rows, :]
        if slot > 0:
            return strip_ref[slot - 1, chan, rows, :]
        value = strip_own[chan, rows, :]
        outside = (depth + row_starts[slot] >= TH) & (tile == tiles - 1)
        return jnp.where(outside, 0.0, value)

    def scans(slots):
        number = len(slots)
        exit_re, exit_im = [], []
        for slot in slots:
            damping = jnp.exp(-patch(slot, 1))
            sn, cs = sin_cos(patch(slot, 0))
            tre = damping * cs
            tim = damping * sn
            trans_ref[slot, 0] = tre
            trans_ref[slot, 1] = tim
            exit_re.append(probe_re * tre - probe_im * tim)
            exit_im.append(probe_re * tim + probe_im * tre)
        data = jnp.concatenate(
            [jnp.concatenate(exit_re, axis=1), jnp.concatenate(exit_im, axis=1)], axis=0
        )
        wide = left_product(m1h_ref[...], m1l_ref[...], data)
        wide = jnp.concatenate(
            [
                jnp.concatenate(
                    [wide[:PIX, j * PIX : (j + 1) * PIX], wide[PIX:, j * PIX : (j + 1) * PIX]],
                    axis=1,
                )
                for j in range(number)
            ],
            axis=0,
        )
        far = right_product(wide, m2h_ref[...], m2l_ref[...])
        residual = []
        for j, slot in enumerate(slots):
            rows = far[j * PIX : (j + 1) * PIX]
            re, im = rows[:, :PIX], rows[:, PIX:]
            live = tile > 0 if slot == PREV else slot < count_ref[0, 0]
            inverse = lax.rsqrt(jnp.maximum(re * re + im * im, AMP_FLOOR * AMP_FLOOR))
            factor = jnp.where(live, 1.0 - amp_ref[slot] * inverse, 0.0)
            residual.append(jnp.concatenate([re * factor, im * factor], axis=1))
        back = right_product(jnp.concatenate(residual, axis=0), m1h_ref[...], m1l_ref[...])
        tall = jnp.concatenate(
            [
                jnp.concatenate([back[j * PIX : (j + 1) * PIX, :PIX] for j in range(number)], axis=1),
                jnp.concatenate([back[j * PIX : (j + 1) * PIX, PIX:] for j in range(number)], axis=1),
            ],
            axis=0,
        )
        grad = left_product(m2h_ref[...], m2l_ref[...], tall)
        for j, slot in enumerate(slots):
            bre = grad[:PIX, j * PIX : (j + 1) * PIX]
            bim = grad[PIX:, j * PIX : (j + 1) * PIX]
            gre = probe_re * bre + probe_im * bim
            gim = probe_re * bim - probe_im * bre
            tre = trans_ref[slot, 0]
            tim = trans_ref[slot, 1]
            at = TH if slot == 0 else 0 if slot == PREV else SHIFT
            bottom = SHIFT if slot != PREV else TH + SHIFT
            start = (SHIFT if slot in range(1, SLOTS) else TH) - row_starts[slot]
            for chan, value in enumerate((tre * gim - tim * gre, -(tre * gre + tim * gim))):
                if at:
                    back_ref[slot, chan, :at] = jnp.zeros((at, PIX), F32)
                back_ref[slot, chan, at : at + PIX] = value
                back_ref[slot, chan, at + PIX : at + PIX + bottom] = jnp.zeros((bottom, PIX), F32)
                placed = back_ref[slot, chan, pl.ds(start, TH), :]
                for z in range(LAYERS):
                    first_row = chan * CHAN_ROWS + z * TH
                    rolled_ref[slot, first_row : first_row + TH] = pltpu.roll(
                        placed, offsets[slot][z], 1
                    )

    def receive_strips():
        for item in strip_edges:
            item.wait_recv()
        for chan in range(2):
            strip_own[chan, lower, :] = edge_in[chan, 0].astype(F32)
            strip_prev[chan, upper, :] = edge_in[chan, 1].astype(F32)

    far_strip = lax.rem(tile, 2) == 1

    @pl.when(far_strip)
    def _():
        scans((1, 2, 3))
        receive_strips()
        scans((0, PREV))

    @pl.when(jnp.logical_not(far_strip))
    def _():
        receive_strips()
        scans((1, 2, 3, 0, PREV))

    line = lax.broadcasted_iota(jnp.int32, (8, COLS), 1)

    def contribution(target, chunk):
        begin, size = CHUNKS[chunk]
        pieces = []
        for z_start in range(0, BLOCK_ROWS, TH):
            low, high = max(begin, z_start), min(begin + size, z_start + TH)
            if low >= high:
                continue
            z = (z_start // TH) % LAYERS
            total = None
            for slot in range(STRIPS):
                offset = offsets[slot][z]
                in_first = target == firsts[slot][z]
                in_second = target == seconds[slot][z]
                least = jnp.where(in_first, offset, jnp.where(in_second, 0, COLS))
                most = jnp.where(in_first, COLS, jnp.where(in_second, offset, 0))
                inside = (lane[: high - low] >= least) & (lane[: high - low] < most)
                value = jnp.where(inside, rolled_ref[slot, low:high], 0.0)
                total = value if total is None else total + value
            pieces.append(total)
        return jnp.concatenate(pieces, axis=0) if len(pieces) > 1 else pieces[0]

    def reduce_copy(step, chunk, to_right):
        rows = pl.ds(*CHUNKS[chunk])
        if to_right:
            return remote(
                out_r.at[step, rows, :],
                in_r.at[step, rows, :],
                send_r2.at[step, chunk],
                recv_r2.at[step, chunk],
                {"ang": right},
            )
        return remote(
            out_l.at[step, rows, :],
            in_l.at[step, rows, :],
            send_l2.at[step, chunk],
            recv_l2.at[step, chunk],
            {"ang": left},
        )

    def reduced(step, to_right):
        if step > 0:
            return ALL_CHUNKS
        return FIRST_HALF if to_right else SECOND_HALF

    def prepare(step, chunk, to_right):
        if to_right:
            target = lax.rem(me + half - step, blocks)
        else:
            target = lax.rem(me - half + step + blocks, blocks)
        way = 0 if to_right else 1
        ready_ref[step % 2, way, pl.ds(*CHUNKS[chunk]), :] = contribution(target, chunk)

    def advance(step, chunk, to_right):
        rows = pl.ds(*CHUNKS[chunk])
        going, coming = (out_r, in_r) if to_right else (out_l, in_l)
        total = ready_ref[step % 2, 0 if to_right else 1, rows, :]
        if step > 0 and chunk in reduced(step - 1, to_right):
            reduce_copy(step - 1, chunk, to_right).wait_recv()
            total = total + coming[step - 1, rows, :].astype(F32)
        going[step, rows, :] = total.astype(BF16)
        item = reduce_copy(step, chunk, to_right)
        item.start()
        started.append(item)

    own = []
    for step in range(half):
        for index in range(len(ALL_CHUNKS)):
            for to_right in (True, False):
                chunk = ALL_CHUNKS[index if to_right else -1 - index]
                if chunk in reduced(step, to_right):
                    if step == 0:
                        prepare(step, chunk, to_right)
                    advance(step, chunk, to_right)
                if step > 0 and step + 1 < half:
                    prepare(step + 1, chunk, to_right)
            if step == half - 1:
                own.append(contribution(me, ALL_CHUNKS[index]))
        if step == 0:
            for index in range(len(ALL_CHUNKS)):
                for to_right in (True, False):
                    prepare(1, ALL_CHUNKS[index if to_right else -1 - index], to_right)
    own = jnp.concatenate(own, axis=0)
    for chan, chunks in ((0, FIRST_HALF), (1, SECOND_HALF)):
        for chunk in chunks:
            for to_right in (True, False):
                reduce_copy(half - 1, chunk, to_right).wait_recv()
        rows = pl.ds(chan * CHAN_ROWS, CHAN_ROWS)
        total = in_r[half - 1, rows, :].astype(F32) + in_l[half - 1, rows, :].astype(F32)
        total = total + own[chan * CHAN_ROWS : (chan + 1) * CHAN_ROWS]
        for z in range(LAYERS):
            out_ref[chan, pl.ds(z, TH, stride=LAYERS), :] = total[z * TH : (z + 1) * TH]
    for item in started:
        item.wait_send()


VMEM = pl.BlockSpec(memory_space=pltpu.VMEM)
HBM = pl.BlockSpec(memory_space=pltpu.HBM)


def on_device(delta_obj, beta_obj, layer_shifts, field, amplitudes, positions, counts):
    blocks = lax.axis_size("ang")
    tiles = lax.axis_size("rows")
    half = blocks // 2
    table = pltpu.VMEM((2 * PIX, 2 * PIX), BF16)
    stage = pltpu.VMEM((half, BLOCK_ROWS, COLS), BF16)
    ring_sems = pltpu.SemaphoreType.DMA((half, len(CHUNKS)))
    pos = jnp.swapaxes(positions, 1, 2)
    grad = pl.pallas_call(
        functools.partial(kernel, blocks, tiles),
        out_shape=jax.ShapeDtypeStruct((2, CHAN_ROWS, COLS), F32),
        in_specs=[HBM] * 11,
        out_specs=VMEM,
        scratch_shapes=[
            pltpu.VMEM((2, CHAN_ROWS, COLS), F32),
            pltpu.VMEM((2, PIX, PIX), F32),
            pltpu.VMEM((STRIPS, PIX, PIX), F32),
            table,
            table,
            table,
            table,
            pltpu.SMEM((LAYERS, blocks), jnp.int32),
            pltpu.SMEM((1, 2, SLOTS), jnp.int32),
            pltpu.SMEM((1, 1), jnp.int32),
            pltpu.VMEM((2, SLOTS), jnp.int32),
            pltpu.SMEM((2, SLOTS), jnp.int32),
            pltpu.VMEM((blocks, BLOCK_ROWS, COLS), BF16),
            pltpu.VMEM((SLOTS - 1, 2, TH, PIX), F32),
            pltpu.VMEM((2, 2 * TH, PIX), F32),
            pltpu.VMEM((2, 2 * TH, PIX), F32),
            pltpu.VMEM((STRIPS, 2, PIX, PIX), F32),
            pltpu.VMEM((STRIPS, 2, 2 * TH, PIX), F32),
            pltpu.VMEM((STRIPS, BLOCK_ROWS, COLS), F32),
            stage,
            stage,
            stage,
            stage,
            pltpu.SemaphoreType.DMA((12,)),
            pltpu.SemaphoreType.DMA((6,)),
            pltpu.SemaphoreType.DMA((6,)),
        ]
        + [ring_sems] * 8
        + [pltpu.VMEM((2, 2, BLOCK_ROWS, COLS), F32)]
        + [pltpu.VMEM((2, 2, PIX, PIX), BF16)] * 2,
        compiler_params=pltpu.CompilerParams(
            vmem_limit_bytes=50331648, collective_id=0, has_side_effects=True
        ),
    )(
        *(
            pltpu.with_memory_space_constraint(value, pltpu.HBM)
            for value in (
                delta_obj.reshape(CHAN_ROWS, COLS),
                beta_obj.reshape(CHAN_ROWS, COLS),
                field,
                amplitudes,
                *(jnp.asarray(m) for m in dft_constants()),
                layer_shifts.T,
                pos,
            )
        ),
        counts,
    )
    shape = (TH, LAYERS, COLS)
    return (grad[0].reshape(shape), grad[1].reshape(shape))


def solution(mesh):
    placed = (
        P("rows", None, "ang"),
        P("rows", None, "ang"),
        P(),
        P(),
        P("ang", "rows", None, None),
        P("ang", "rows", None),
        P("ang", "rows"),
    )
    return jax.shard_map(
        on_device,
        mesh=mesh,
        in_specs=placed,
        out_specs=(P("rows", None, "ang"), P("rows", None, "ang")),
        check_vma=False,
    )
```
